256 devices in a mesh: row: 16 (over z, core), col: 16 (over y, x).
Axes of the slice: x: 4, y: 4, z: 8, core: 2. Of those that a mesh axis runs over, the one named last changes fastest.
Arguments:
- correlation: float32 [2, 8192, 8192], P(None, 'row', 'col'), may hold values from -16 to 32, as said below
- fock: float32 [2, 8192, 8192], P(None, 'row', 'col'), may hold values from -6 to 6, as said below
Outputs:
- reduced_correlation: float32 [2, 8192, 8192], P(None, 'row', 'col')
- transformed_fock: float32 [2, 8192, 8192], P(None, 'row', 'col')
- panel_factor: float32 [2, 8192, 96], P(None, 'row')
The draws below stay inside these ranges and needn't reach their ends.
Inputs may be any that keep to these rules, and one draw needn't show every extreme that they name: `correlation`: hermitian and positive definite: part 0 is symmetric, part 1 antisymmetric. `fock`: Hermitian: part 0 is symmetric, part 1 antisymmetric.
All inputs are finite; a program needn't handle non-finite values.
Results may differ from the reference program's by a relative error of at most 0.00013.
Values sent between devices are 32-bit elements; how exact they have to be, the bound alone decides.
A program may use at most 128 MiB of HBM per device.

```python
import math
import jax
import jax.numpy as jnp
from jax import lax

ORDER = 8192
PANEL = 96


def draw_correlation(key, part):
    first = jax.random.fold_in(key, 11)
    second = jax.random.fold_in(key, 12)
    third = jax.random.fold_in(key, 13)
    fourth = jax.random.fold_in(key, 14)
    fifth = jax.random.fold_in(key, 15)
    spread = math.sqrt(2.5 / PANEL)
    basis_real = spread * jnp.clip(jax.random.normal(fourth, (ORDER, PANEL), jnp.float32), -4.0, 4.0)
    basis_imag = spread * jnp.clip(jax.random.normal(fifth, (ORDER, PANEL), jnp.float32), -4.0, 4.0)
    real_noise = jnp.clip(jax.random.normal(first, (ORDER, ORDER), jnp.float32), -5.0, 5.0)
    imag_noise = jnp.clip(jax.random.normal(second, (ORDER, ORDER), jnp.float32), -5.0, 5.0)
    highest = lax.Precision.HIGHEST
    gram_real = jnp.dot(basis_real, basis_real.T, precision=highest) + jnp.dot(basis_imag, basis_imag.T, precision=highest)
    gram_imag = jnp.dot(basis_imag, basis_real.T, precision=highest) - jnp.dot(basis_real, basis_imag.T, precision=highest)
    weight = 0.25 / math.sqrt(ORDER)
    diagonal = jax.random.uniform(third, (ORDER,), jnp.float32, 2.0, 5.0)
    index = jnp.arange(ORDER)
    distance = jnp.abs(index[:, None] - index[None, :]).astype(jnp.float32)
    banded = 8.0 * jnp.exp(distance * math.log(0.6))
    real_part = 0.5 * (gram_real + gram_real.T) + (real_noise + real_noise.T) * weight + jnp.diag(diagonal) + banded
    imag_part = 0.5 * (gram_imag - gram_imag.T) + (imag_noise - imag_noise.T) * weight
    return jnp.stack([real_part, imag_part])


def draw_fock(key, part):
    first = jax.random.fold_in(key, 21)
    second = jax.random.fold_in(key, 22)
    real_noise = jnp.clip(jax.random.normal(first, (ORDER, ORDER), jnp.float32), -5.0, 5.0)
    imag_noise = jnp.clip(jax.random.normal(second, (ORDER, ORDER), jnp.float32), -5.0, 5.0)
    real_part = 0.5 * (real_noise + real_noise.T)
    imag_part = 0.5 * (imag_noise - imag_noise.T)
    return jnp.stack([real_part, imag_part])


def setup_inputs(seed: int = 0) -> dict:
    arg_keys = jax.random.split(jax.random.key(seed), 3)
    return {
        "correlation": draw_correlation(jax.random.fold_in(arg_keys[2], 71), 0),
        "fock": draw_fock(jax.random.fold_in(arg_keys[2], 71), 0),
    }


highest = lax.Precision.HIGHEST

def complex_product(left_real, left_imag, right_real, right_imag):
    real_part = jnp.dot(left_real, right_real, precision=highest) - jnp.dot(left_imag, right_imag, precision=highest)
    imag_part = jnp.dot(left_real, right_imag, precision=highest) + jnp.dot(left_imag, right_real, precision=highest)
    return (real_part, imag_part)

def embed_real(real_part, imag_part):
    count = real_part.shape[0]
    upper = jnp.stack([real_part, -imag_part], axis=-1)
    lower = jnp.stack([imag_part, real_part], axis=-1)
    return jnp.stack([upper, lower], axis=1).reshape(2 * count, 2 * count)

def triangular_inverse(real_part, imag_part):
    embedded = embed_real(real_part, imag_part)
    identity = jnp.eye(embedded.shape[0], dtype=embedded.dtype)
    inverse = jax.scipy.linalg.solve_triangular(embedded, identity, lower=True)
    return (inverse[0::2, 0::2], inverse[1::2, 0::2])

def cholesky_inverse(real_part, imag_part):
    factor = jnp.linalg.cholesky(embed_real(real_part, imag_part))
    return triangular_inverse(factor[0::2, 0::2], factor[1::2, 0::2])

def reference(correlation, fock):
    over_real, over_imag = (correlation[0], correlation[1])
    inverse_real, inverse_imag = cholesky_inverse(over_real[:PANEL, :PANEL], over_imag[:PANEL, :PANEL])
    factor_real, factor_imag = complex_product(over_real[:, :PANEL], over_imag[:, :PANEL], inverse_real.T, -inverse_imag.T)
    outer_real, outer_imag = complex_product(factor_real, factor_imag, factor_real.T, -factor_imag.T)
    reduced = jnp.stack([over_real - outer_real, over_imag - outer_imag])
    unit = jnp.eye(ORDER, PANEL, dtype=jnp.float32)
    trans_real, trans_imag = complex_product(unit - factor_real, -factor_imag, inverse_real, inverse_imag)
    fock_real, fock_imag = (fock[0], fock[1])
    step_real, step_imag = complex_product(trans_real, trans_imag, fock_real[:PANEL], fock_imag[:PANEL])
    partly_real = fock_real + step_real
    partly_imag = fock_imag + step_imag
    back_real, back_imag = complex_product(partly_real[:, :PANEL], partly_imag[:, :PANEL], trans_real.T, -trans_imag.T)
    transformed = jnp.stack([partly_real + back_real, partly_imag + back_imag])
    return (reduced, transformed, jnp.stack([factor_real, factor_imag]))
```

```python
import jax
import jax.numpy as jnp
from jax import lax
from jax.experimental import pallas as pl
from jax.experimental.pallas import tpu as pltpu
from jax.sharding import PartitionSpec as P

PANEL = 96
LANES = 128
MESH = pl.DeviceIdType.MESH

INTO = (-1, 0, 0, 0, 2, 1, 0, 0, 2, 1, 1, 0, 2, 3, 3, 0)
DEPTH = (0, 1, 2, 3, 3, 2, 3, 4, 4, 3, 4, 5, 3, 2, 3, 4)
STEP = ((1, 0), (0, 1), (-1, 0), (0, -1))

TREE_CHUNKS = 8
TREE_ROWS = 32
CHAIN_CHUNKS = 12
CHAIN_ROWS = 16
TREE_LAG = 3
CHAIN_LAG = 3
SLOTS = 25


def rotated(x, y, turns):
    for _ in range(turns % 4):
        x, y = -y % 4, x % 4
    return x, y


def tree_tables():
    depth = [[0] * 16 for _ in range(4)]
    send = [[-1] * 16 for _ in range(4)]
    for tree in range(4):
        for chip in range(16):
            x, y = rotated(chip % 4, chip // 4, -tree)
            depth[tree][chip] = DEPTH[y * 4 + x]
            if chip:
                way = (INTO[y * 4 + x] + tree) % 4
                px, py = (chip % 4 - STEP[way][0]) % 4, (chip // 4 - STEP[way][1]) % 4
                assert send[way][py * 4 + px] == -1
                send[way][py * 4 + px] = tree
    return depth, send


def lookup(index, table):
    value = jnp.int32(0)
    for k, entry in enumerate(table):
        if entry:
            value = value + jnp.where(index == k, jnp.int32(entry), jnp.int32(0))
    return value


def spread(corr, fock, rowp, colp, small, wr, wi, dv, local_sem, tree_send, tree_recv, chain_send, chain_recv, small_send, small_recv):
    r, c = lax.axis_index("row"), lax.axis_index("col")
    z, core = r // 2, r % 2
    y, x = c // 4, c % 4
    root = (r == 0) & (c == 0)
    depth_table, send_table = tree_tables()

    def along_x(step):
        return (r, 4 * y + (x + step) % 4)

    def along_y(step):
        return (r, 4 * ((y + step) % 4) + x)

    def along_z(step):
        return (2 * ((z + step) % 8) + core, c)

    partner = (r + 1 - 2 * core, c)

    barrier = pltpu.get_barrier_semaphore()
    greeted = [along_x(s) for s in (1, 2, 3)] + [along_y(s) for s in (1, 2, 3)] + [along_z(s) for s in range(1, 8)] + [partner]
    for peer in greeted:
        pl.semaphore_signal(barrier, inc=1, device_id=peer, device_id_type=MESH)

    row_copies = [pltpu.make_async_copy(src.at[:, :, pl.ds(0, LANES)], rowp.at[i], local_sem.at[i]) for i, src in enumerate((corr, fock))]
    col_copies = [pltpu.make_async_copy(src.at[:, pl.ds(0, PANEL), :], colp.at[i], local_sem.at[2 + i]) for i, src in enumerate((corr, fock))]

    @pl.when(c == 0)
    def _():
        for copy in row_copies:
            copy.start()

    @pl.when(r == 0)
    def _():
        for copy in col_copies:
            copy.start()

    @pl.when(c == 0)
    def _():
        for copy in row_copies:
            copy.wait()

    @pl.when(r == 0)
    def _():
        for copy in col_copies:
            copy.wait()

    neighbours = (along_x(1), along_y(1), along_x(3), along_y(3))

    def tree_copy(tree, chunk, way):
        rows = pl.ds(pl.multiple_of(LANES * tree + TREE_ROWS * (chunk % 4), TREE_ROWS), TREE_ROWS)
        part = rowp.at[chunk // 4, :, rows, :]
        return pltpu.make_async_remote_copy(
            src_ref=part, dst_ref=part, send_sem=tree_send.at[way, chunk], recv_sem=tree_recv.at[tree, chunk],
            device_id=neighbours[way], device_id_type=MESH)

    chain_peers = (along_z(1), along_z(7), partner)

    def chain_copy(chunk, way):
        rows = pl.ds(pl.multiple_of(CHAIN_ROWS * (chunk % 6), CHAIN_ROWS), CHAIN_ROWS)
        part = colp.at[chunk // 6, :, rows, :]
        return pltpu.make_async_remote_copy(
            src_ref=part, dst_ref=part, send_sem=chain_send.at[way, chunk], recv_sem=chain_recv.at[chunk],
            device_id=chain_peers[way], device_id_type=MESH)

    def small_copy(which, index, peer):
        return pltpu.make_async_remote_copy(
            src_ref=small.at[which], dst_ref=small.at[which], send_sem=small_send.at[which, index],
            recv_sem=small_recv.at[which], device_id=peer, device_id_type=MESH)

    def small_groups(which):
        far_z = [small_copy(which, i, along_z(s)) for i, s in enumerate((4, 3, 5, 2, 6, 1, 7))]
        far_x = [small_copy(which, 7 + i, along_x(s)) for i, s in enumerate((2, 1, 3))]
        far_y = [small_copy(which, 10 + i, along_y(s)) for i, s in enumerate((2, 1, 3))]
        near = [small_copy(which, 13, partner)]
        return (((root, far_z), ((c == 0) & (core == 0), far_x), ((y == 0) & (core == 0), far_y), (core == 0, near)))

    def small_forward(which):
        for condition, copies in small_groups(which):
            @pl.when(condition)
            def _():
                for copy in copies:
                    copy.start()

    def small_event(which):
        small_copy(which, 13, partner).wait_recv()
        small_forward(which)

    send_tree = [lookup(c, [entry + 1 for entry in send_table[way]]) - 1 for way in range(4)]
    chain_up = (core == 0) & (z < 4)
    chain_down = (core == 0) & ((z == 0) | (z > 5))
    chain_ways = (chain_up, chain_down, core == 0)

    @pl.when(root)
    def _():
        lane = lax.broadcasted_iota(jnp.int32, (PANEL, LANES), 1)
        row = lax.broadcasted_iota(jnp.int32, (PANEL, LANES), 0)
        inside = lane < PANEL
        wr[...] = jnp.where(inside, rowp[0, 0, pl.ds(0, PANEL), :], 0.0)
        wi[...] = jnp.zeros_like(wi)
        wi[pl.ds(0, PANEL), :] = jnp.where(inside, rowp[0, 1, pl.ds(0, PANEL), :], 0.0)
        head_real = rowp[1, 0, pl.ds(0, PANEL), :]
        head_imag = rowp[1, 1, pl.ds(0, PANEL), :]
        small[0] = jnp.where(inside, jnp.where(lane <= row, head_real, head_imag), 0.0)

        def eliminate(block, carry):
            for j in range(8):
                k = block * 8 + j
                at = lane == j
                row_real = wr[pl.ds(k, 1), :]
                row_imag = wi[pl.ds(k, 1), :]
                pivot = jnp.broadcast_to(row_real[:, j:j + 1], (1, LANES))
                dv[pl.ds(k, 1), :] = pivot
                scale = 1.0 / pivot
                here = at[0:1, :]
                row_real = jnp.where(here, scale, row_real * scale)
                row_imag = jnp.where(here, 0.0, row_imag * scale)
                real, imag = wr[...], wi[pl.ds(0, PANEL), :]
                below = row > k
                col_real = jnp.where(below, jnp.broadcast_to(real[:, j:j + 1], (PANEL, LANES)), 0.0)
                col_imag = jnp.where(below, jnp.broadcast_to(imag[:, j:j + 1], (PANEL, LANES)), 0.0)
                wr[...] = jnp.where(at, 0.0, real) - (col_real * row_real - col_imag * row_imag)
                wi[pl.ds(0, PANEL), :] = jnp.where(at, 0.0, imag) - (col_real * row_imag + col_imag * row_real)
            wr[...] = pltpu.roll(wr[...], LANES - 8, 1)
            wi[pl.ds(0, PANEL), :] = pltpu.roll(wi[pl.ds(0, PANEL), :], LANES - 8, 1)

            @pl.when(block == 4)
            def _():
                pl.semaphore_wait(barrier, len(greeted))
                small_forward(0)

            @pl.when((block >= 5) & (block < 9))
            def _():
                for i in range(2):
                    for way in range(4):
                        tree_copy(way, 2 * (block - 5) + i, way).start()
                for i in range(3):
                    for way in range(3):
                        chain_copy(3 * (block - 5) + i, way).start()

            return carry

        lax.fori_loop(0, PANEL // 8, eliminate, 0)
        pivots = dv[...]
        scale = lax.rsqrt(pivots)
        scale = scale * (1.5 - 0.5 * pivots * scale * scale)
        eye = jnp.where(lane == row, 1.0, 0.0)
        inverse_real = (pltpu.roll(wr[...], PANEL, 1) + eye) * scale
        wi[pl.ds(0, PANEL), :] = pltpu.roll(wi[pl.ds(0, PANEL), :], PANEL, 1) * scale
        small[1] = inverse_real + wi[...].T[0:PANEL, :]
        small_forward(1)

    @pl.when(jnp.logical_not(root))
    def _():
        pl.semaphore_wait(barrier, len(greeted))
        depth = [lookup(c, depth_table[tree]) for tree in range(4)]
        chain_depth = jnp.where(z <= 4, z, 8 - z)
        small_slot = jnp.where(c == 0, 7, jnp.where(y == 0, 11, 15))

        def slot(s, carry):
            for tree in range(4):
                chunk = s - TREE_LAG * depth[tree]

                @pl.when((chunk >= 0) & (chunk < TREE_CHUNKS))
                def _():
                    @pl.when(c != 0)
                    def _():
                        tree_copy(tree, chunk, 0).wait_recv()

                    for way in range(4):
                        @pl.when(send_tree[way] == tree)
                        def _():
                            tree_copy(tree, chunk, way).start()

            link = s - CHAIN_LAG * chain_depth

            @pl.when((core == 0) & (link >= 0) & (link < CHAIN_CHUNKS))
            def _():
                @pl.when(z != 0)
                def _():
                    chain_copy(link, 0).wait_recv()

                for way in range(3):
                    @pl.when(chain_ways[way])
                    def _():
                        chain_copy(link, way).start()

            @pl.when(s == small_slot)
            def _():
                small_event(0)

            return carry

        lax.fori_loop(0, SLOTS, slot, 0)
        small_event(1)

        @pl.when(core == 1)
        def _():
            def arrived(chunk, carry):
                chain_copy(chunk, 2).wait_recv()
                return carry

            lax.fori_loop(0, CHAIN_CHUNKS, arrived, 0)

    for way in range(4):
        @pl.when(send_tree[way] >= 0)
        def _():
            def sent(chunk, carry):
                tree_copy(0, chunk, way).wait_send()
                return carry

            lax.fori_loop(0, TREE_CHUNKS, sent, 0)

    for way in range(3):
        @pl.when(chain_ways[way])
        def _():
            def sent(chunk, carry):
                chain_copy(chunk, way).wait_send()
                return carry

            lax.fori_loop(0, CHAIN_CHUNKS, sent, 0)

    for which in range(2):
        for condition, copies in small_groups(which):
            @pl.when(condition)
            def _():
                for copy in copies:
                    copy.wait_send()


def halves(value):
    high = value.astype(jnp.bfloat16)
    return high, (value - high.astype(jnp.float32)).astype(jnp.bfloat16)


def product(left, right):
    (left_high, left_low), (right_high, right_low) = left, right

    def dot(a, b):
        return jnp.dot(a, b, preferred_element_type=jnp.float32)

    return dot(left_high, right_high) + (dot(left_low, right_high) + dot(left_high, right_low))


def block_matrix(a, b, c, d):
    return jnp.concatenate([jnp.concatenate([a, b], axis=1), jnp.concatenate([c, d], axis=1)], axis=0)


TILE = 128


def update(corr, fock, rowp, colp, small, over, transformed, panel, cbuf, fbuf, pbuf, over_left, over_right, fock_left, fock_right, in_sem, out_sem, panel_sem):
    r, c = lax.axis_index("row"), lax.axis_index("col")
    loads = [pltpu.make_async_copy(src, dst, in_sem.at[i]) for i, (src, dst) in enumerate(((corr, cbuf), (fock, fbuf)))]
    for load in loads:
        load.start()

    size = rowp.shape[2]
    width = colp.shape[3]
    row = lax.broadcasted_iota(jnp.int32, (LANES, LANES), 0)
    col = lax.broadcasted_iota(jnp.int32, (LANES, LANES), 1)
    rest = jnp.zeros((LANES - PANEL, LANES), jnp.float32)
    packed = jnp.concatenate([small[1], rest], axis=0)
    turned = packed.T
    inv_real = jnp.where(row >= col, packed, 0.0)
    inv_imag = jnp.where(row > col, turned, 0.0)
    inv_real_t = jnp.where(row <= col, turned, 0.0)
    inv_imag_t = jnp.where(row < col, packed, 0.0)
    right_adjoint = halves(block_matrix(inv_real_t, -inv_imag_t, inv_imag_t, inv_real_t))
    right_inverse = halves(block_matrix(inv_real, inv_imag, -inv_imag, inv_real))
    left_inverse = halves(block_matrix(inv_real, -inv_imag, inv_imag, inv_real))
    left_adjoint = halves(block_matrix(inv_real_t, inv_imag_t, -inv_imag_t, inv_real_t))

    gap = jnp.zeros((LANES - PANEL, width), jnp.float32)

    def top(which):
        return jnp.concatenate([colp[which, 0], gap, colp[which, 1], gap], axis=0)

    factor = product(halves(jnp.concatenate([rowp[0, 0], rowp[0, 1]], axis=1)), right_adjoint)
    pbuf[0] = factor[:, 0:PANEL]
    pbuf[1] = factor[:, LANES:LANES + PANEL]
    panel_out = pltpu.make_async_copy(pbuf, panel, panel_sem)
    panel_out.start()
    over_left[0], over_left[1] = halves(factor)
    across = product(left_inverse, halves(top(0)))

    def right_side(value):
        real, imag = value[0:LANES], value[LANES:2 * LANES]
        return block_matrix(real, imag, -imag, real)

    over_right[0], over_right[1] = halves(right_side(across))

    out_copies = []

    def outer_tiles(left, right, buffer, target, which, sign):
        for tile in range(size // TILE):
            rows = pl.ds(tile * TILE, TILE)
            change = product((left[0, rows, :], left[1, rows, :]), (right[0], right[1]))
            for part in range(2):
                piece = change[:, part * width:(part + 1) * width]
                old = buffer[part, rows, :]
                buffer[part, rows, :] = old + piece if sign > 0 else old - piece
            copy = pltpu.make_async_copy(buffer.at[:, rows, :], target.at[:, rows, :], out_sem.at[which, tile])
            copy.start()
            out_copies.append(copy)

    loads[0].wait()
    outer_tiles(over_left, over_right, cbuf, over, 0, -1)

    wide_row = lax.broadcasted_iota(jnp.int32, (size, 2 * LANES), 0) + r * size
    wide_lane = lax.broadcasted_iota(jnp.int32, (size, 2 * LANES), 1)
    unit = jnp.where((wide_row == wide_lane) & (wide_lane < PANEL), 1.0, 0.0)
    trans = product(halves(unit - factor), right_inverse)
    fock_left[0, :, 0:2 * LANES], fock_left[1, :, 0:2 * LANES] = halves(trans)
    fock_left[0, :, 2 * LANES:4 * LANES], fock_left[1, :, 2 * LANES:4 * LANES] = halves(jnp.concatenate([rowp[1, 0], rowp[1, 1]], axis=1))
    tall_row = lax.broadcasted_iota(jnp.int32, (2 * LANES, width), 0)
    tall_lane = lax.broadcasted_iota(jnp.int32, (2 * LANES, width), 1) + c * width
    unit = jnp.where((tall_row == tall_lane) & (tall_row < PANEL), 1.0, 0.0)
    trans_across = product(left_adjoint, halves(unit - across))

    packed = jnp.concatenate([small[0], rest], axis=0)
    turned = packed.T
    head_real = jnp.where(row >= col, packed, turned)
    head_imag = jnp.where(row < col, packed, jnp.where(row > col, -turned, 0.0))
    head = halves(block_matrix(head_real, -head_imag, head_imag, head_real))
    middle = top(1) + product(head, halves(trans_across))
    fock_right[0, 0:2 * LANES, :], fock_right[1, 0:2 * LANES, :] = halves(right_side(middle))
    fock_right[0, 2 * LANES:4 * LANES, :], fock_right[1, 2 * LANES:4 * LANES, :] = halves(right_side(trans_across))

    loads[1].wait()
    outer_tiles(fock_left, fock_right, fbuf, transformed, 1, 1)
    panel_out.wait()
    for copy in out_copies:
        copy.wait()


def shards(correlation, fock):
    rows, cols = correlation.shape[1:]
    f32, bf16 = jnp.float32, jnp.bfloat16
    hbm, vmem = pl.BlockSpec(memory_space=pl.ANY), pl.BlockSpec(memory_space=pltpu.VMEM)
    dma = pltpu.SemaphoreType.DMA
    rowp, colp, small = pl.pallas_call(
        spread,
        name="spread",
        out_shape=(
            jax.ShapeDtypeStruct((2, 2, rows, LANES), f32),
            jax.ShapeDtypeStruct((2, 2, PANEL, cols), f32),
            jax.ShapeDtypeStruct((2, PANEL, LANES), f32),
        ),
        in_specs=[hbm, hbm],
        out_specs=(vmem, vmem, vmem),
        scratch_shapes=[
            pltpu.VMEM((PANEL, LANES), f32),
            pltpu.VMEM((LANES, LANES), f32),
            pltpu.VMEM((PANEL, LANES), f32),
            dma((4,)),
            dma((4, TREE_CHUNKS)),
            dma((4, TREE_CHUNKS)),
            dma((3, CHAIN_CHUNKS)),
            dma((CHAIN_CHUNKS,)),
            dma((2, 14)),
            dma((2,)),
        ],
        compiler_params=pltpu.CompilerParams(collective_id=0, has_side_effects=True),
    )(correlation, fock)
    return pl.pallas_call(
        update,
        name="update",
        out_shape=(
            jax.ShapeDtypeStruct((2, rows, cols), f32),
            jax.ShapeDtypeStruct((2, rows, cols), f32),
            jax.ShapeDtypeStruct((2, rows, PANEL), f32),
        ),
        in_specs=[hbm, hbm, vmem, vmem, vmem],
        out_specs=(hbm, hbm, hbm),
        scratch_shapes=[
            pltpu.VMEM((2, rows, cols), f32),
            pltpu.VMEM((2, rows, cols), f32),
            pltpu.VMEM((2, rows, PANEL), f32),
            pltpu.VMEM((2, rows, 2 * LANES), bf16),
            pltpu.VMEM((2, 2 * LANES, 2 * cols), bf16),
            pltpu.VMEM((2, rows, 4 * LANES), bf16),
            pltpu.VMEM((2, 4 * LANES, 2 * cols), bf16),
            dma((2,)),
            dma((2, rows // TILE)),
            dma,
        ],
        compiler_params=pltpu.CompilerParams(vmem_limit_bytes=48 * 1024 * 1024),
    )(correlation, fock, rowp, colp, small)


def solution(mesh):
    in_specs = (P(None, "row", "col"), P(None, "row", "col"))
    out_specs = (P(None, "row", "col"), P(None, "row", "col"), P(None, "row", None))
    return jax.shard_map(shards, mesh=mesh, in_specs=in_specs, out_specs=out_specs, check_vma=False)
```

```python
import jax
import jax.numpy as jnp
from jax import lax
from jax.experimental import pallas as pl
from jax.experimental.pallas import tpu as pltpu
from jax.sharding import PartitionSpec as P

PANEL = 96
LANES = 128
MESH = pl.DeviceIdType.MESH

INTO = (-1, 0, 0, 0, 2, 1, 0, 0, 2, 1, 1, 0, 2, 3, 3, 0)
DEPTH = (0, 1, 2, 3, 3, 2, 3, 4, 4, 3, 4, 5, 3, 2, 3, 4)
STEP = ((1, 0), (0, 1), (-1, 0), (0, -1))

TREE_ROWS = 32
TREE_CHUNKS = 2 * LANES // TREE_ROWS
CHAIN_ROWS = 16
CHAIN_CHUNKS = 2 * PANEL // CHAIN_ROWS
TREE_LAG = 5
CHAIN_LAG = 5
CHAIN_START = 3
DOWN_START = 4
STAGE_SLOTS = 5
SMALL_SLOT = 9
SLOTS = max(5 * TREE_LAG + TREE_CHUNKS, 4 * CHAIN_LAG + CHAIN_CHUNKS + CHAIN_START + DOWN_START, 4 * STAGE_SLOTS + SMALL_SLOT + 1)
GREET_AT = 46
HEAD_AT = 78


def rotated(x, y, turns):
    for _ in range(turns % 4):
        x, y = -y % 4, x % 4
    return x, y


def tree_tables():
    depth = [[0] * 16 for _ in range(4)]
    send = [[-1] * 16 for _ in range(4)]
    for tree in range(4):
        for chip in range(16):
            x, y = rotated(chip % 4, chip // 4, -tree)
            depth[tree][chip] = DEPTH[y * 4 + x]
            if chip:
                way = (INTO[y * 4 + x] + tree) % 4
                px, py = (chip % 4 - STEP[way][0]) % 4, (chip // 4 - STEP[way][1]) % 4
                assert send[way][py * 4 + px] == -1
                send[way][py * 4 + px] = tree
    return depth, send


def lookup(index, table):
    value = jnp.int32(0)
    for k, entry in enumerate(table):
        if entry:
            value = value + jnp.where(index == k, jnp.int32(entry), jnp.int32(0))
    return value


def spread(corr, fock, rowp, colp, small, wr, wi, dv, head, local_sem, tree_send, tree_recv, chain_send, chain_recv, small_send, small_recv, chain_ready, chain_ready_down, small_ready):
    r, c = lax.axis_index("row"), lax.axis_index("col")
    z, core = r // 2, r % 2
    y, x = c // 4, c % 4
    root = (r == 0) & (c == 0)
    depth_table, send_table = tree_tables()

    def along_x(step):
        return (r, 4 * y + (x + step) % 4)

    def along_y(step):
        return (r, 4 * ((y + step) % 4) + x)

    def along_z(step):
        return (2 * ((z + step) % 8) + core, c)

    partner = (r + 1 - 2 * core, c)

    barrier = pltpu.get_barrier_semaphore()
    greeted = [along_x(s) for s in (1, 2, 3)] + [along_y(s) for s in (1, 2, 3)] + [partner]
    for peer in greeted:
        pl.semaphore_signal(barrier, inc=1, device_id=peer, device_id_type=MESH)

    on_chain = core == jnp.where(c == 0, 1, 0)
    edge = (c == 0) & (core == 0)
    chain_up, chain_down = on_chain & (z < 4), on_chain & ((z == 0) | (z > 5))
    z_greetings = (
        (chain_up, 1), (chain_down, 7),
        (edge & ((z == 0) | (z == 3)), 1), (edge & (z == 0), 2), (edge & (z == 0), 3),
        (edge & ((z == 0) | (z == 6)), 7), (edge & (z == 0), 6))
    for condition, step in z_greetings:
        @pl.when(condition)
        def _():
            pl.semaphore_signal(barrier, inc=1, device_id=along_z(step), device_id_type=MESH)

    heard = len(greeted) + jnp.where((z > 0) & (on_chain | edge), 1, 0)

    def answer():
        pl.semaphore_wait(barrier, heard)

        @pl.when(on_chain & (z > 0) & (z <= 4))
        def _():
            pl.semaphore_signal(chain_ready, inc=1, device_id=along_z(7), device_id_type=MESH)

        @pl.when(on_chain & (z > 4))
        def _():
            pl.semaphore_signal(chain_ready_down, inc=1, device_id=along_z(1), device_id_type=MESH)

        @pl.when(edge & (z > 0))
        def _():
            back = jnp.where((z == 1) | (z == 4), 7, jnp.where(z == 2, 6, jnp.where(z == 3, 5, jnp.where(z == 6, 2, 1))))
            pl.semaphore_signal(small_ready, inc=1, device_id=along_z(back), device_id_type=MESH)

    head_copies = [pltpu.make_async_copy(corr.at[:, pl.ds(0, PANEL), pl.ds(0, LANES)], head, local_sem.at[4])]
    row_copies = [pltpu.make_async_copy(src.at[:, :, pl.ds(0, LANES)], rowp.at[i], local_sem.at[i]) for i, src in enumerate((corr, fock))]
    col_copies = [pltpu.make_async_copy(src.at[:, pl.ds(0, PANEL), :], colp.at[i], local_sem.at[2 + i]) for i, src in enumerate((corr, fock))]

    @pl.when(root)
    def _():
        for copy in head_copies:
            copy.start()

    @pl.when(c == 0)
    def _():
        for copy in row_copies:
            copy.start()

    @pl.when(r == 0)
    def _():
        for copy in col_copies:
            copy.start()

    def loaded():
        @pl.when(c == 0)
        def _():
            for copy in row_copies:
                copy.wait()

        @pl.when(r == 0)
        def _():
            for copy in col_copies:
                copy.wait()

    neighbours = (along_x(1), along_y(1), along_x(3), along_y(3))

    def tree_copy(tree, chunk, way):
        rows = pl.ds(pl.multiple_of(LANES * tree + TREE_ROWS * (chunk % (TREE_CHUNKS // 2)), TREE_ROWS), TREE_ROWS)
        part = rowp.at[chunk // (TREE_CHUNKS // 2), :, rows, :]
        return pltpu.make_async_remote_copy(
            src_ref=part, dst_ref=part, send_sem=tree_send.at[way, chunk], recv_sem=tree_recv.at[tree, chunk],
            device_id=neighbours[way], device_id_type=MESH)

    chain_peers = (along_z(1), along_z(7), partner)

    def chain_copy(chunk, way):
        rows = pl.ds(pl.multiple_of(CHAIN_ROWS * (chunk % (CHAIN_CHUNKS // 2)), CHAIN_ROWS), CHAIN_ROWS)
        part = colp.at[chunk // (CHAIN_CHUNKS // 2), :, rows, :]
        return pltpu.make_async_remote_copy(
            src_ref=part, dst_ref=part, send_sem=chain_send.at[way, chunk], recv_sem=chain_recv.at[chunk],
            device_id=chain_peers[way], device_id_type=MESH)

    def small_copy(which, index, peer):
        return pltpu.make_async_remote_copy(
            src_ref=small.at[which], dst_ref=small.at[which], send_sem=small_send.at[which, index],
            recv_sem=small_recv.at[which], device_id=peer, device_id_type=MESH)

    def small_groups(which):
        z_steps = [small_copy(which, i, along_z(s)) for i, s in enumerate((3, 6, 2, 7, 1))]
        x_steps = [small_copy(which, 5 + i, along_x(s)) for i, s in enumerate((2, 1, 3))]
        y_steps = [small_copy(which, 8 + i, along_y(s)) for i, s in enumerate((2, 1, 3))]
        return (
            (root, z_steps), (edge & (z == 3), [z_steps[4]]), (edge & (z == 6), [z_steps[3]]),
            (edge, x_steps), ((y == 0) & (core == 0), y_steps), (core == 0, [small_copy(which, 11, partner)]))

    def small_forward(which):
        for condition, copies in small_groups(which):
            @pl.when(condition)
            def _():
                for copy in copies:
                    copy.start()

    def small_event(which):
        small_copy(which, 11, partner).wait_recv()
        small_forward(which)

    send_tree = [lookup(c, [entry + 1 for entry in send_table[way]]) - 1 for way in range(4)]
    chain_ways = (chain_up, chain_down, root | (on_chain & jnp.logical_not((r == 1) & (c == 0))))

    @pl.when(root)
    def _():
        lane = lax.broadcasted_iota(jnp.int32, (PANEL, LANES), 1)
        row = lax.broadcasted_iota(jnp.int32, (PANEL, LANES), 0)
        inside = lane < PANEL
        for copy in head_copies:
            copy.wait()

        tile_lane = lax.broadcasted_iota(jnp.int32, (8, LANES), 1)
        tile_row = lax.broadcasted_iota(jnp.int32, (8, LANES), 0)
        count = PANEL // 8
        real = [head[0, pl.ds(8 * t, 8), :] for t in range(count)]
        imag = [head[1, pl.ds(8 * t, 8), :] for t in range(count)]

        def down(value, j):
            return jnp.broadcast_to(value[j:j + 1, :], (8, LANES))

        def across(value, j):
            return jnp.broadcast_to(value[:, j:j + 1], (8, LANES))

        for k in range(0, PANEL, 2):
            tile, j = k // 8, k % 8
            first, second = tile_lane == k, tile_lane == k + 1
            col_a = [(across(real[t], k), across(imag[t], k)) for t in range(tile, count)]
            col_b = [(across(real[t], k + 1), across(imag[t], k + 1)) for t in range(tile, count)]
            pivot_a = down(col_a[0][0], j)
            off_real, off_imag = down(col_a[0][0], j + 1), down(col_a[0][1], j + 1)
            inv_a = 1.0 / pivot_a
            low_real, low_imag = off_real * inv_a, off_imag * inv_a
            pivot_b = down(col_b[0][0], j + 1) - (off_real * low_real + off_imag * low_imag)
            inv_b = 1.0 / pivot_b
            both = first | second
            a_real = jnp.where(both, jnp.where(first, 1.0, 0.0), down(real[tile], j))
            a_imag = jnp.where(both, 0.0, down(imag[tile], j))
            b_real = jnp.where(both, jnp.where(second, 1.0, 0.0), down(real[tile], j + 1))
            b_imag = jnp.where(both, 0.0, down(imag[tile], j + 1))
            b_real, b_imag = (
                b_real - (low_real * a_real - low_imag * a_imag), b_imag - (low_real * a_imag + low_imag * a_real))
            wb_real, wb_imag = b_real * inv_b, b_imag * inv_b
            wa_real = a_real * inv_a - (low_real * wb_real + low_imag * wb_imag)
            wa_imag = a_imag * inv_a - (low_real * wb_imag - low_imag * wb_real)
            for t in range(tile, count):
                (ar, ai), (br, bi) = col_a[t - tile], col_b[t - tile]
                next_real = jnp.where(both, 0.0, real[t]) - ((ar * wa_real - ai * wa_imag) + (br * wb_real - bi * wb_imag))
                next_imag = jnp.where(both, 0.0, imag[t]) - ((ar * wa_imag + ai * wa_real) + (br * wb_imag + bi * wb_real))
                if t == tile:
                    keep = tile_row < j
                    next_real = jnp.where(keep, real[t], jnp.where(tile_row == j, a_real, jnp.where(tile_row == j + 1, b_real, next_real)))
                    next_imag = jnp.where(keep, imag[t], jnp.where(tile_row == j, a_imag, jnp.where(tile_row == j + 1, b_imag, next_imag)))
                real[t], imag[t] = next_real, next_imag
            dv[pl.ds(k, 1), :] = pivot_a[0:1, :]
            dv[pl.ds(k + 1, 1), :] = pivot_b[0:1, :]

            if k == GREET_AT:
                loaded()
                answer()
                for chunk in range(TREE_CHUNKS):
                    for way in range(4):
                        tree_copy(way, chunk, way).start()
                for chunk in range(CHAIN_CHUNKS):
                    chain_copy(chunk, 2).start()

            if k == HEAD_AT:
                head_real = rowp[1, 0, pl.ds(0, PANEL), :]
                head_imag = rowp[1, 1, pl.ds(0, PANEL), :]
                small[0] = jnp.where(inside, jnp.where(lane <= row, head_real, head_imag), 0.0)
                pl.semaphore_wait(small_ready, 5)
                small_forward(0)

        pivots = dv[...]
        scale = lax.rsqrt(pivots)
        scale = scale * (1.5 - 0.5 * pivots * scale * scale)
        for t in range(count):
            lower = tile_lane <= tile_row + 8 * t
            rows = pl.ds(8 * t, 8)
            wr[rows, :] = jnp.where(lower, real[t], 0.0)
            wi[rows, :] = jnp.where(lower, imag[t], 0.0)
        wi[pl.ds(0, PANEL), :] = wi[pl.ds(0, PANEL), :] * scale
        wi[pl.ds(PANEL, LANES - PANEL), :] = jnp.zeros((LANES - PANEL, LANES), jnp.float32)
        small[1] = wr[...] * scale + wi[...].T[0:PANEL, :]
        small_forward(1)

    @pl.when(jnp.logical_not(root))
    def _():
        loaded()
        answer()
        depth = [lookup(c, depth_table[tree]) for tree in range(4)]
        way_start = [
            jnp.where((c == 0) | (send_tree[way] < 0), SLOTS, TREE_LAG * lookup(c, [
                depth_table[tree][chip] if tree >= 0 else 0 for chip, tree in enumerate(send_table[way])]))
            for way in range(4)]
        chain_depth = jnp.where(z <= 4, z, 8 - z)
        chain_now = (chain_up, on_chain & (z > 5), chain_ways[2])
        chain_depth_slots = CHAIN_LAG * chain_depth + CHAIN_START + jnp.where(z > 4, DOWN_START, 0)
        stage = jnp.where(z == 0, 0, jnp.where((z == 4) | (z == 5), 2, 1)) + jnp.where(x == 0, 0, 1) + jnp.where(y == 0, 0, 1)
        small_slot = SMALL_SLOT + STAGE_SLOTS * stage

        @pl.when(c == 0)
        def _():
            def source(chunk, carry):
                for way in range(4):
                    tree_copy(way, chunk, way).start()
                return carry

            lax.fori_loop(0, TREE_CHUNKS, source, 0)

        def slot(s, carry):
            for tree in range(4):
                chunk = s - TREE_LAG * depth[tree]

                @pl.when((c != 0) & (chunk >= 0) & (chunk < TREE_CHUNKS))
                def _():
                    tree_copy(tree, chunk, 0).wait_recv()

            for way in range(4):
                onward = s - way_start[way]

                @pl.when((onward >= 0) & (onward < TREE_CHUNKS))
                def _():
                    tree_copy(send_tree[way], onward, way).start()

            link = s - chain_depth_slots

            @pl.when(on_chain & (link >= 0) & (link < CHAIN_CHUNKS))
            def _():
                @pl.when((z != 0) | (c == 0))
                def _():
                    chain_copy(link, 0).wait_recv()

                @pl.when((link == 0) & chain_up)
                def _():
                    pl.semaphore_wait(chain_ready, 1)

                @pl.when((link == 0) & (z > 5))
                def _():
                    pl.semaphore_wait(chain_ready_down, 1)

                for way in range(3):
                    @pl.when(chain_now[way])
                    def _():
                        chain_copy(link, way).start()

            link_down = s - CHAIN_START - DOWN_START

            @pl.when(on_chain & (z == 0) & (link_down >= 0) & (link_down < CHAIN_CHUNKS))
            def _():
                @pl.when(link_down == 0)
                def _():
                    pl.semaphore_wait(chain_ready_down, 1)

                chain_copy(link_down, 1).start()

            @pl.when(s == small_slot)
            def _():
                @pl.when(edge & ((z == 3) | (z == 6)))
                def _():
                    pl.semaphore_wait(small_ready, 1)

                small_event(0)
                small_event(1)

            return carry

        lax.fori_loop(0, SLOTS, slot, 0)

        @pl.when(jnp.logical_not(on_chain))
        def _():
            def arrived(chunk, carry):
                chain_copy(chunk, 2).wait_recv()
                return carry

            lax.fori_loop(0, CHAIN_CHUNKS, arrived, 0)

    for way in range(4):
        @pl.when(send_tree[way] >= 0)
        def _():
            def sent(chunk, carry):
                tree_copy(0, chunk, way).wait_send()
                return carry

            lax.fori_loop(0, TREE_CHUNKS, sent, 0)

    for way in range(3):
        @pl.when(chain_ways[way])
        def _():
            def sent(chunk, carry):
                chain_copy(chunk, way).wait_send()
                return carry

            lax.fori_loop(0, CHAIN_CHUNKS, sent, 0)

    for which in range(2):
        for condition, copies in small_groups(which):
            @pl.when(condition)
            def _():
                for copy in copies:
                    copy.wait_send()


def halves(value):
    high = value.astype(jnp.bfloat16)
    return high, (value - high.astype(jnp.float32)).astype(jnp.bfloat16)


def product(left, right):
    (left_high, left_low), (right_high, right_low) = left, right

    def dot(a, b):
        return jnp.dot(a, b, preferred_element_type=jnp.float32)

    return dot(left_high, right_high) + (dot(left_low, right_high) + dot(left_high, right_low))


def block_matrix(a, b, c, d):
    return jnp.concatenate([jnp.concatenate([a, b], axis=1), jnp.concatenate([c, d], axis=1)], axis=0)


TILE = 256


def update(
    corr, fock, rowp_in, colp_in, small_in, over, transformed, panel, rowp, colp, small, cbuf, fbuf, pbuf,
    over_left, over_right, fock_left, fock_right, in_sem, out_sem, panel_sem,
):
    r, c = lax.axis_index("row"), lax.axis_index("col")
    pairs = (
        (small_in, small), (rowp_in.at[0], rowp.at[0]), (colp_in.at[0], colp.at[0]), (corr, cbuf),
        (rowp_in.at[1], rowp.at[1]), (colp_in.at[1], colp.at[1]), (fock, fbuf))
    loads = [pltpu.make_async_copy(src, dst, in_sem.at[i]) for i, (src, dst) in enumerate(pairs)]
    for load in loads:
        load.start()
    loads[0].wait()

    size = rowp.shape[2]
    width = colp.shape[3]
    row = lax.broadcasted_iota(jnp.int32, (LANES, LANES), 0)
    col = lax.broadcasted_iota(jnp.int32, (LANES, LANES), 1)
    rest = jnp.zeros((LANES - PANEL, LANES), jnp.float32)
    packed = jnp.concatenate([small[1], rest], axis=0)
    turned = packed.T
    inv_real = jnp.where(row >= col, packed, 0.0)
    inv_imag = jnp.where(row > col, turned, 0.0)
    inv_real_t = jnp.where(row <= col, turned, 0.0)
    inv_imag_t = jnp.where(row < col, packed, 0.0)
    right_adjoint = halves(block_matrix(inv_real_t, -inv_imag_t, inv_imag_t, inv_real_t))
    right_inverse = halves(block_matrix(inv_real, inv_imag, -inv_imag, inv_real))
    left_inverse = halves(block_matrix(inv_real, -inv_imag, inv_imag, inv_real))
    left_adjoint = halves(block_matrix(inv_real_t, inv_imag_t, -inv_imag_t, inv_real_t))

    gap = jnp.zeros((LANES - PANEL, width), jnp.float32)

    def top(which):
        return jnp.concatenate([colp[which, 0], gap, colp[which, 1], gap], axis=0)

    loads[1].wait()
    factor = product(halves(jnp.concatenate([rowp[0, 0], rowp[0, 1]], axis=1)), right_adjoint)
    pbuf[0] = factor[:, 0:LANES].T[0:PANEL]
    pbuf[1] = factor[:, LANES:2 * LANES].T[0:PANEL]
    panel_out = pltpu.make_async_copy(pbuf, panel, panel_sem)
    panel_out.start()
    over_left[0], over_left[1] = halves(factor)
    loads[2].wait()
    across = product(left_inverse, halves(top(0)))

    def right_side(value):
        real, imag = value[0:LANES], value[LANES:2 * LANES]
        return block_matrix(real, imag, -imag, real)

    over_right[0], over_right[1] = halves(right_side(across))

    out_copies = []

    def outer_tiles(left, right, buffer, target, which, sign):
        for tile in range(2 * width // TILE):
            part, cols = tile // (width // TILE), pl.ds(tile % (width // TILE) * TILE, TILE)
            columns = pl.ds(tile * TILE, TILE)
            piece = product((left[0], left[1]), (right[0, :, columns], right[1, :, columns]))
            old = buffer[part, :, cols]
            buffer[part, :, cols] = old + piece if sign > 0 else old - piece
            copy = pltpu.make_async_copy(buffer.at[part, :, cols], target.at[part, :, cols], out_sem.at[which, tile])
            copy.start()
            out_copies.append(copy)

    loads[3].wait()
    outer_tiles(over_left, over_right, cbuf, over, 0, -1)

    wide_row = lax.broadcasted_iota(jnp.int32, (size, 2 * LANES), 0) + r * size
    wide_lane = lax.broadcasted_iota(jnp.int32, (size, 2 * LANES), 1)
    unit = jnp.where((wide_row == wide_lane) & (wide_lane < PANEL), 1.0, 0.0)
    trans = product(halves(unit - factor), right_inverse)
    loads[4].wait()
    loads[5].wait()
    fock_left[0, :, 0:2 * LANES], fock_left[1, :, 0:2 * LANES] = halves(trans)
    fock_left[0, :, 2 * LANES:4 * LANES], fock_left[1, :, 2 * LANES:4 * LANES] = halves(jnp.concatenate([rowp[1, 0], rowp[1, 1]], axis=1))
    tall_row = lax.broadcasted_iota(jnp.int32, (2 * LANES, width), 0)
    tall_lane = lax.broadcasted_iota(jnp.int32, (2 * LANES, width), 1) + c * width
    unit = jnp.where((tall_row == tall_lane) & (tall_row < PANEL), 1.0, 0.0)
    trans_across = product(left_adjoint, halves(unit - across))

    packed = jnp.concatenate([small[0], rest], axis=0)
    turned = packed.T
    head_real = jnp.where(row >= col, packed, turned)
    head_imag = jnp.where(row < col, packed, jnp.where(row > col, -turned, 0.0))
    head = halves(block_matrix(head_real, -head_imag, head_imag, head_real))
    middle = top(1) + product(head, halves(trans_across))
    fock_right[0, 0:2 * LANES, :], fock_right[1, 0:2 * LANES, :] = halves(right_side(middle))
    fock_right[0, 2 * LANES:4 * LANES, :], fock_right[1, 2 * LANES:4 * LANES, :] = halves(right_side(trans_across))

    loads[6].wait()
    outer_tiles(fock_left, fock_right, fbuf, transformed, 1, 1)
    panel_out.wait()
    for copy in out_copies:
        copy.wait()


def shards(correlation, fock):
    rows, cols = correlation.shape[1:]
    f32, bf16 = jnp.float32, jnp.bfloat16
    hbm, vmem = pl.BlockSpec(memory_space=pl.ANY), pl.BlockSpec(memory_space=pltpu.VMEM)
    dma = pltpu.SemaphoreType.DMA
    rowp, colp, small = pl.pallas_call(
        spread,
        name="spread",
        out_shape=(
            jax.ShapeDtypeStruct((2, 2, rows, LANES), f32),
            jax.ShapeDtypeStruct((2, 2, PANEL, cols), f32),
            jax.ShapeDtypeStruct((2, PANEL, LANES), f32),
        ),
        in_specs=[hbm, hbm],
        out_specs=(vmem, vmem, vmem),
        scratch_shapes=[
            pltpu.VMEM((PANEL, LANES), f32),
            pltpu.VMEM((LANES, LANES), f32),
            pltpu.VMEM((PANEL, LANES), f32),
            pltpu.VMEM((2, PANEL, LANES), f32),
            dma((5,)),
            dma((4, TREE_CHUNKS)),
            dma((4, TREE_CHUNKS)),
            dma((3, CHAIN_CHUNKS)),
            dma((CHAIN_CHUNKS,)),
            dma((2, 12)),
            dma((2,)),
            pltpu.SemaphoreType.REGULAR,
            pltpu.SemaphoreType.REGULAR,
            pltpu.SemaphoreType.REGULAR,
        ],
        compiler_params=pltpu.CompilerParams(collective_id=0, has_side_effects=True),
    )(correlation, fock)
    reduced, transformed, panel = pl.pallas_call(
        update,
        name="update",
        out_shape=(
            jax.ShapeDtypeStruct((2, rows, cols), f32),
            jax.ShapeDtypeStruct((2, rows, cols), f32),
            jax.ShapeDtypeStruct((2, PANEL, rows), f32),
        ),
        in_specs=[hbm, hbm, hbm, hbm, hbm],
        out_specs=(hbm, hbm, hbm),
        scratch_shapes=[
            pltpu.VMEM((2, 2, rows, LANES), f32),
            pltpu.VMEM((2, 2, PANEL, cols), f32),
            pltpu.VMEM((2, PANEL, LANES), f32),
            pltpu.VMEM((2, rows, cols), f32),
            pltpu.VMEM((2, rows, cols), f32),
            pltpu.VMEM((2, PANEL, rows), f32),
            pltpu.VMEM((2, rows, 2 * LANES), bf16),
            pltpu.VMEM((2, 2 * LANES, 2 * cols), bf16),
            pltpu.VMEM((2, rows, 4 * LANES), bf16),
            pltpu.VMEM((2, 4 * LANES, 2 * cols), bf16),
            dma((7,)),
            dma((2, 2 * cols // TILE)),
            dma,
        ],
        compiler_params=pltpu.CompilerParams(vmem_limit_bytes=65 * 1000 * 1000),
    )(correlation, fock, rowp, colp, small)
    return reduced, transformed, jnp.swapaxes(panel, 1, 2)


def solution(mesh):
    in_specs = (P(None, "row", "col"), P(None, "row", "col"))
    out_specs = (P(None, "row", "col"), P(None, "row", "col"), P(None, "row", None))
    return jax.shard_map(shards, mesh=mesh, in_specs=in_specs, out_specs=out_specs, check_vma=False)
```

```python
import jax
import jax.numpy as jnp
from jax import lax
from jax.experimental import pallas as pl
from jax.experimental.pallas import tpu as pltpu
from jax.sharding import PartitionSpec as P

PANEL = 96
LANES = 128
MESH = pl.DeviceIdType.MESH

INTO = (-1, 0, 0, 0, 2, 1, 0, 0, 2, 1, 1, 0, 2, 3, 3, 0)
DEPTH = (0, 1, 2, 3, 3, 2, 3, 4, 4, 3, 4, 5, 3, 2, 3, 4)
STEP = ((1, 0), (0, 1), (-1, 0), (0, -1))

TREE_ROWS = 32
TREE_CHUNKS = 2 * LANES // TREE_ROWS
CHAIN_ROWS = 16
CHAIN_CHUNKS = 2 * PANEL // CHAIN_ROWS
TREE_LAG = 5
CHAIN_LAG = 4
CHAIN_START = 0
DOWN_START = 4
STAGE_SLOTS = 5
SMALL_SLOT = 9
EARLY_SLOTS = 5
SLOTS = max(5 * TREE_LAG + TREE_CHUNKS, 4 * CHAIN_LAG + CHAIN_CHUNKS + CHAIN_START + DOWN_START, 4 * STAGE_SLOTS + SMALL_SLOT + EARLY_SLOTS + 1)
GREET_AT = 30
HEAD_AT = 78


def rotated(x, y, turns):
    for _ in range(turns % 4):
        x, y = -y % 4, x % 4
    return x, y


def tree_tables():
    depth = [[0] * 16 for _ in range(4)]
    send = [[-1] * 16 for _ in range(4)]
    for tree in range(4):
        for chip in range(16):
            x, y = rotated(chip % 4, chip // 4, -tree)
            depth[tree][chip] = DEPTH[y * 4 + x]
            if chip:
                way = (INTO[y * 4 + x] + tree) % 4
                px, py = (chip % 4 - STEP[way][0]) % 4, (chip // 4 - STEP[way][1]) % 4
                assert send[way][py * 4 + px] == -1
                send[way][py * 4 + px] = tree
    return depth, send


def lookup(index, table):
    value = jnp.int32(0)
    for k, entry in enumerate(table):
        if entry:
            value = value + jnp.where(index == k, jnp.int32(entry), jnp.int32(0))
    return value


def spread(
    corr, fock, rowp_out, colp_out, small_out, rowp, colp, small, wr, wi, dv, head, local_sem, out_sem, tree_send, tree_recv, chain_send, chain_recv, small_send, small_recv, chain_ready, chain_ready_down, small_ready, small_ready_down,
):
    r, c = lax.axis_index("row"), lax.axis_index("col")
    z, core = r // 2, r % 2
    y, x = c // 4, c % 4
    root = (r == 0) & (c == 0)
    depth_table, send_table = tree_tables()

    def along_x(step):
        return (r, 4 * y + (x + step) % 4)

    def along_y(step):
        return (r, 4 * ((y + step) % 4) + x)

    def along_z(step):
        return (2 * ((z + step) % 8) + core, c)

    partner = (r + 1 - 2 * core, c)

    barrier = pltpu.get_barrier_semaphore()
    greeted = [along_x(s) for s in (1, 2, 3)] + [along_y(s) for s in (1, 2, 3)] + [partner]
    for peer in greeted:
        pl.semaphore_signal(barrier, inc=1, device_id=peer, device_id_type=MESH)

    on_chain = core == jnp.where(c == 0, 1, 0)
    edge = (c == 0) & (core == 0)
    chain_up, chain_down = on_chain & (z < 4), on_chain & ((z == 0) | (z > 5))
    z_greetings = (
        (on_chain & (z > 0) & (z < 4), 7), (on_chain & ((z == 5) | (z == 6)), 1),
        (edge & (z == 1), 7), (edge & (z == 2), 6), (edge & (z == 3), 5),
        (on_chain & (z == 3), 1), (on_chain & (z == 0), 7),
        (edge & (z == 3), 1), (edge & (z == 0), 7), (edge & (z == 0), 6), (edge & (z == 6), 7))
    for condition, step in z_greetings:
        @pl.when(condition)
        def _():
            pl.semaphore_signal(barrier, inc=1, device_id=along_z(step), device_id_type=MESH)

    heard = len(greeted) + jnp.where(on_chain & (z != 3) & (z != 5), 1, 0) + jnp.where(on_chain & (z == 7), 1, 0)
    heard = heard + jnp.where(root, 3, 0) + jnp.where(edge & (z > 3), 1, 0)

    def answer():
        pl.semaphore_wait(barrier, heard)

        @pl.when(on_chain & (z == 4))
        def _():
            pl.semaphore_signal(chain_ready, inc=1, device_id=along_z(7), device_id_type=MESH)

        @pl.when(on_chain & (z == 7))
        def _():
            pl.semaphore_signal(chain_ready_down, inc=1, device_id=along_z(1), device_id_type=MESH)

        @pl.when(edge & (z == 4))
        def _():
            pl.semaphore_signal(small_ready, inc=1, device_id=along_z(7), device_id_type=MESH)

        @pl.when(edge & (z > 4))
        def _():
            back = jnp.where(z == 6, 2, 1)
            pl.semaphore_signal(small_ready_down, inc=1, device_id=along_z(back), device_id_type=MESH)

    head_copies = [pltpu.make_async_copy(corr.at[:, pl.ds(0, PANEL), pl.ds(0, LANES)], head, local_sem.at[4])]
    row_copies = [pltpu.make_async_copy(src.at[:, :, pl.ds(0, LANES)], rowp.at[i], local_sem.at[i]) for i, src in enumerate((corr, fock))]
    col_copies = [pltpu.make_async_copy(src.at[:, pl.ds(0, PANEL), :], colp.at[i], local_sem.at[2 + i]) for i, src in enumerate((corr, fock))]

    @pl.when(root)
    def _():
        for copy in head_copies:
            copy.start()

    @pl.when(c == 0)
    def _():
        for copy in row_copies:
            copy.start()

    @pl.when(r == 0)
    def _():
        for copy in col_copies:
            copy.start()

    def loaded():
        @pl.when(c == 0)
        def _():
            for copy in row_copies:
                copy.wait()

        @pl.when(r == 0)
        def _():
            for copy in col_copies:
                copy.wait()

    neighbours = (along_x(1), along_y(1), along_x(3), along_y(3))

    def tree_copy(tree, chunk, way):
        rows = pl.ds(pl.multiple_of(LANES * tree + TREE_ROWS * (chunk % (TREE_CHUNKS // 2)), TREE_ROWS), TREE_ROWS)
        part = rowp.at[chunk // (TREE_CHUNKS // 2), :, rows, :]
        return pltpu.make_async_remote_copy(
            src_ref=part, dst_ref=part, send_sem=tree_send.at[way, chunk], recv_sem=tree_recv.at[tree, chunk],
            device_id=neighbours[way], device_id_type=MESH)

    chain_peers = (along_z(1), along_z(7), partner)

    def chain_copy(chunk, way):
        rows = pl.ds(pl.multiple_of(CHAIN_ROWS * (chunk % (CHAIN_CHUNKS // 2)), CHAIN_ROWS), CHAIN_ROWS)
        part = colp.at[chunk // (CHAIN_CHUNKS // 2), :, rows, :]
        return pltpu.make_async_remote_copy(
            src_ref=part, dst_ref=part, send_sem=chain_send.at[way, chunk], recv_sem=chain_recv.at[chunk],
            device_id=chain_peers[way], device_id_type=MESH)

    def small_copy(which, index, peer):
        return pltpu.make_async_remote_copy(
            src_ref=small.at[which], dst_ref=small.at[which], send_sem=small_send.at[which, index],
            recv_sem=small_recv.at[which], device_id=peer, device_id_type=MESH)

    def small_groups(which):
        z_steps = [small_copy(which, i, along_z(s)) for i, s in enumerate((3, 6, 2, 7, 1))]
        x_steps = [small_copy(which, 5 + i, along_x(s)) for i, s in enumerate((2, 1, 3))]
        y_steps = [small_copy(which, 8 + i, along_y(s)) for i, s in enumerate((2, 1, 3))]
        return (
            (root, [z_steps[0], z_steps[2], z_steps[4]]), (edge & (z == 3), [z_steps[4]]), (edge & (z == 6), [z_steps[3]]),
            (edge, x_steps), ((y == 0) & (core == 0), y_steps), (core == 0, [small_copy(which, 11, partner)]),
            (root, [z_steps[1], z_steps[3]]))

    def small_forward(which):
        for condition, copies in small_groups(which)[:-1]:
            @pl.when(condition)
            def _():
                for copy in copies:
                    copy.start()

    def small_event(which):
        small_copy(which, 11, partner).wait_recv()
        small_forward(which)

    send_tree = [lookup(c, [entry + 1 for entry in send_table[way]]) - 1 for way in range(4)]
    chain_ways = (chain_up, chain_down, root | (on_chain & jnp.logical_not((r == 1) & (c == 0))))

    @pl.when(root)
    def _():
        lane = lax.broadcasted_iota(jnp.int32, (PANEL, LANES), 1)
        row = lax.broadcasted_iota(jnp.int32, (PANEL, LANES), 0)
        inside = lane < PANEL
        for copy in head_copies:
            copy.wait()

        tile_lane = lax.broadcasted_iota(jnp.int32, (8, LANES), 1)
        tile_row = lax.broadcasted_iota(jnp.int32, (8, LANES), 0)
        count = PANEL // 8
        real = [head[0, pl.ds(8 * t, 8), :] for t in range(count)]
        imag = [head[1, pl.ds(8 * t, 8), :] for t in range(count)]

        def down(value, j):
            return jnp.broadcast_to(value[j:j + 1, :], (8, LANES))

        def across(value, j):
            return jnp.broadcast_to(value[:, j:j + 1], (8, LANES))

        for k in range(0, PANEL, 2):
            tile, j = k // 8, k % 8
            first, second = tile_lane == k, tile_lane == k + 1
            col_a = [(across(real[t], k), across(imag[t], k)) for t in range(tile, count)]
            col_b = [(across(real[t], k + 1), across(imag[t], k + 1)) for t in range(tile, count)]
            pivot_a = down(col_a[0][0], j)
            off_real, off_imag = down(col_a[0][0], j + 1), down(col_a[0][1], j + 1)
            inv_a = 1.0 / pivot_a
            low_real, low_imag = off_real * inv_a, off_imag * inv_a
            pivot_b = down(col_b[0][0], j + 1) - (off_real * low_real + off_imag * low_imag)
            inv_b = 1.0 / pivot_b
            both = first | second
            a_real = jnp.where(both, jnp.where(first, 1.0, 0.0), down(real[tile], j))
            a_imag = jnp.where(both, 0.0, down(imag[tile], j))
            b_real = jnp.where(both, jnp.where(second, 1.0, 0.0), down(real[tile], j + 1))
            b_imag = jnp.where(both, 0.0, down(imag[tile], j + 1))
            b_real, b_imag = (
                b_real - (low_real * a_real - low_imag * a_imag), b_imag - (low_real * a_imag + low_imag * a_real))
            wb_real, wb_imag = b_real * inv_b, b_imag * inv_b
            wa_real = a_real * inv_a - (low_real * wb_real + low_imag * wb_imag)
            wa_imag = a_imag * inv_a - (low_real * wb_imag - low_imag * wb_real)
            for t in range(tile, count):
                (ar, ai), (br, bi) = col_a[t - tile], col_b[t - tile]
                next_real = jnp.where(both, 0.0, real[t]) - ((ar * wa_real - ai * wa_imag) + (br * wb_real - bi * wb_imag))
                next_imag = jnp.where(both, 0.0, imag[t]) - ((ar * wa_imag + ai * wa_real) + (br * wb_imag + bi * wb_real))
                if t == tile:
                    keep = tile_row < j
                    next_real = jnp.where(keep, real[t], jnp.where(tile_row == j, a_real, jnp.where(tile_row == j + 1, b_real, next_real)))
                    next_imag = jnp.where(keep, imag[t], jnp.where(tile_row == j, a_imag, jnp.where(tile_row == j + 1, b_imag, next_imag)))
                real[t], imag[t] = next_real, next_imag
            dv[pl.ds(k, 1), :] = pivot_a[0:1, :]
            dv[pl.ds(k + 1, 1), :] = pivot_b[0:1, :]

            if k == GREET_AT:
                loaded()
                answer()
                for chunk in range(TREE_CHUNKS):
                    for way in range(4):
                        tree_copy(way, chunk, way).start()
                for chunk in range(CHAIN_CHUNKS):
                    chain_copy(chunk, 2).start()

            if k == HEAD_AT:
                head_real = rowp[1, 0, pl.ds(0, PANEL), :]
                head_imag = rowp[1, 1, pl.ds(0, PANEL), :]
                small[0] = jnp.where(inside, jnp.where(lane <= row, head_real, head_imag), 0.0)
                small_forward(0)

        pivots = dv[...]
        scale = lax.rsqrt(pivots)
        scale = scale * (1.5 - 0.5 * pivots * scale * scale)
        for t in range(count):
            lower = tile_lane <= tile_row + 8 * t
            rows = pl.ds(8 * t, 8)
            wr[rows, :] = jnp.where(lower, real[t], 0.0)
            wi[rows, :] = jnp.where(lower, imag[t], 0.0)
        wi[pl.ds(0, PANEL), :] = wi[pl.ds(0, PANEL), :] * scale
        wi[pl.ds(PANEL, LANES - PANEL), :] = jnp.zeros((LANES - PANEL, LANES), jnp.float32)
        small[1] = wr[...] * scale + wi[...].T[0:PANEL, :]
        small_forward(1)
        pl.semaphore_wait(small_ready_down, 2)
        for which in (1, 0):
            for copy in small_groups(which)[-1][1]:
                copy.start()

    @pl.when(jnp.logical_not(root))
    def _():
        loaded()
        answer()
        depth = [lookup(c, depth_table[tree]) for tree in range(4)]
        way_start = [
            jnp.where((c == 0) | (send_tree[way] < 0), SLOTS, TREE_LAG * lookup(c, [
                depth_table[tree][chip] if tree >= 0 else 0 for chip, tree in enumerate(send_table[way])]))
            for way in range(4)]
        chain_depth = jnp.where(z <= 4, z, 8 - z)
        chain_now = (chain_up, on_chain & (z > 5), chain_ways[2])
        chain_depth_slots = CHAIN_LAG * chain_depth + CHAIN_START + jnp.where(z > 4, DOWN_START, 0)
        stage = jnp.where(z == 0, 0, jnp.where((z == 4) | (z == 5), 2, 1)) + jnp.where(x == 0, 0, 1) + jnp.where(y == 0, 0, 1)
        small_slot = SMALL_SLOT + STAGE_SLOTS * stage + jnp.where(z < 4, EARLY_SLOTS, 0)

        @pl.when(c == 0)
        def _():
            def source(chunk, carry):
                for way in range(4):
                    tree_copy(way, chunk, way).start()
                return carry

            lax.fori_loop(0, TREE_CHUNKS, source, 0)

        def slot(s, carry):
            for tree in range(4):
                chunk = s - TREE_LAG * depth[tree]

                @pl.when((c != 0) & (chunk >= 0) & (chunk < TREE_CHUNKS))
                def _():
                    tree_copy(tree, chunk, 0).wait_recv()

            for way in range(4):
                onward = s - way_start[way]

                @pl.when((onward >= 0) & (onward < TREE_CHUNKS))
                def _():
                    tree_copy(send_tree[way], onward, way).start()

            link = s - chain_depth_slots

            @pl.when(on_chain & (link >= 0) & (link < CHAIN_CHUNKS))
            def _():
                @pl.when((z != 0) | (c == 0))
                def _():
                    chain_copy(link, 0).wait_recv()

                @pl.when((link == 0) & (z == 3))
                def _():
                    pl.semaphore_wait(chain_ready, 1)

                for way in range(3):
                    @pl.when(chain_now[way])
                    def _():
                        chain_copy(link, way).start()

            link_down = s - CHAIN_START - DOWN_START

            @pl.when(on_chain & (z == 0) & (link_down >= 0) & (link_down < CHAIN_CHUNKS))
            def _():
                @pl.when(link_down == 0)
                def _():
                    pl.semaphore_wait(chain_ready_down, 1)

                chain_copy(link_down, 1).start()

            @pl.when(s == small_slot)
            def _():
                @pl.when(edge & (z == 3))
                def _():
                    pl.semaphore_wait(small_ready, 1)

                @pl.when(edge & (z == 6))
                def _():
                    pl.semaphore_wait(small_ready_down, 1)

                small_event(0)
                small_event(1)

            return carry

        lax.fori_loop(0, SLOTS, slot, 0)

        @pl.when(jnp.logical_not(on_chain))
        def _():
            def arrived(chunk, carry):
                chain_copy(chunk, 2).wait_recv()
                return carry

            lax.fori_loop(0, CHAIN_CHUNKS, arrived, 0)

    flushes = [
        pltpu.make_async_copy(src, dst, out_sem.at[i])
        for i, (src, dst) in enumerate(((small, small_out), (rowp, rowp_out), (colp, colp_out)))]
    for flush in flushes:
        flush.start()

    for way in range(4):
        @pl.when(send_tree[way] >= 0)
        def _():
            def sent(chunk, carry):
                tree_copy(0, chunk, way).wait_send()
                return carry

            lax.fori_loop(0, TREE_CHUNKS, sent, 0)

    for way in range(3):
        @pl.when(chain_ways[way])
        def _():
            def sent(chunk, carry):
                chain_copy(chunk, way).wait_send()
                return carry

            lax.fori_loop(0, CHAIN_CHUNKS, sent, 0)

    for which in range(2):
        for condition, copies in small_groups(which):
            @pl.when(condition)
            def _():
                for copy in copies:
                    copy.wait_send()

    for flush in flushes:
        flush.wait()


def halves(value):
    high = value.astype(jnp.bfloat16)
    return high, (value - high.astype(jnp.float32)).astype(jnp.bfloat16)


def product(left, right):
    (left_high, left_low), (right_high, right_low) = left, right

    def dot(a, b):
        return jnp.dot(a, b, preferred_element_type=jnp.float32)

    return dot(left_high, right_high) + (dot(left_low, right_high) + dot(left_high, right_low))


def block_matrix(a, b, c, d):
    return jnp.concatenate([jnp.concatenate([a, b], axis=1), jnp.concatenate([c, d], axis=1)], axis=0)


TILE = 256


def update(
    corr, fock, rowp_in, colp_in, small_in, over, transformed, panel, rowp, colp, small, cbuf, fbuf, pbuf,
    over_left, over_right, fock_left, fock_right, in_sem, out_sem, panel_sem,
):
    r, c = lax.axis_index("row"), lax.axis_index("col")
    pairs = (
        (small_in, small), (rowp_in.at[0], rowp.at[0]), (colp_in.at[0], colp.at[0]), (corr, cbuf),
        (rowp_in.at[1], rowp.at[1]), (colp_in.at[1], colp.at[1]), (fock, fbuf))
    loads = [pltpu.make_async_copy(src, dst, in_sem.at[i]) for i, (src, dst) in enumerate(pairs)]
    for load in loads:
        load.start()
    loads[0].wait()

    size = rowp.shape[2]
    width = colp.shape[3]
    row = lax.broadcasted_iota(jnp.int32, (LANES, LANES), 0)
    col = lax.broadcasted_iota(jnp.int32, (LANES, LANES), 1)
    rest = jnp.zeros((LANES - PANEL, LANES), jnp.float32)
    packed = jnp.concatenate([small[1], rest], axis=0)
    turned = packed.T
    inv_real = jnp.where(row >= col, packed, 0.0)
    inv_imag = jnp.where(row > col, turned, 0.0)
    inv_real_t = jnp.where(row <= col, turned, 0.0)
    inv_imag_t = jnp.where(row < col, packed, 0.0)
    right_adjoint = halves(block_matrix(inv_real_t, -inv_imag_t, inv_imag_t, inv_real_t))
    right_inverse = halves(block_matrix(inv_real, inv_imag, -inv_imag, inv_real))
    left_inverse = halves(block_matrix(inv_real, -inv_imag, inv_imag, inv_real))
    left_adjoint = halves(block_matrix(inv_real_t, inv_imag_t, -inv_imag_t, inv_real_t))

    gap = jnp.zeros((LANES - PANEL, width), jnp.float32)

    def top(which):
        return jnp.concatenate([colp[which, 0], gap, colp[which, 1], gap], axis=0)

    loads[1].wait()
    factor = product(halves(jnp.concatenate([rowp[0, 0], rowp[0, 1]], axis=1)), right_adjoint)
    pbuf[0] = factor[:, 0:LANES].T[0:PANEL]
    pbuf[1] = factor[:, LANES:2 * LANES].T[0:PANEL]
    panel_out = pltpu.make_async_copy(pbuf, panel, panel_sem)
    panel_out.start()
    over_left[0], over_left[1] = halves(factor)
    loads[2].wait()
    across = product(left_inverse, halves(top(0)))

    def right_side(value):
        real, imag = value[0:LANES], value[LANES:2 * LANES]
        return block_matrix(real, imag, -imag, real)

    over_right[0], over_right[1] = halves(right_side(across))

    out_copies = []

    def outer_tiles(left, right, buffer, target, which, sign):
        for tile in range(2 * width // TILE):
            part, cols = tile // (width // TILE), pl.ds(tile % (width // TILE) * TILE, TILE)
            columns = pl.ds(tile * TILE, TILE)
            piece = product((left[0], left[1]), (right[0, :, columns], right[1, :, columns]))
            old = buffer[part, :, cols]
            buffer[part, :, cols] = old + piece if sign > 0 else old - piece
            copy = pltpu.make_async_copy(buffer.at[part, :, cols], target.at[part, :, cols], out_sem.at[which, tile])
            copy.start()
            out_copies.append(copy)

    loads[3].wait()
    outer_tiles(over_left, over_right, cbuf, over, 0, -1)

    wide_row = lax.broadcasted_iota(jnp.int32, (size, 2 * LANES), 0) + r * size
    wide_lane = lax.broadcasted_iota(jnp.int32, (size, 2 * LANES), 1)
    unit = jnp.where((wide_row == wide_lane) & (wide_lane < PANEL), 1.0, 0.0)
    trans = product(halves(unit - factor), right_inverse)
    loads[4].wait()
    loads[5].wait()
    left_real = jnp.concatenate([trans[:, 0:LANES], rowp[1, 0]], axis=1)
    left_imag = jnp.concatenate([trans[:, LANES:2 * LANES], rowp[1, 1]], axis=1)
    for i, value in enumerate((left_real, left_imag, left_real + left_imag)):
        fock_left[0, i], fock_left[1, i] = halves(value)
    tall_row = lax.broadcasted_iota(jnp.int32, (2 * LANES, width), 0)
    tall_lane = lax.broadcasted_iota(jnp.int32, (2 * LANES, width), 1) + c * width
    unit = jnp.where((tall_row == tall_lane) & (tall_row < PANEL), 1.0, 0.0)
    trans_across = product(left_adjoint, halves(unit - across))

    packed = jnp.concatenate([small[0], rest], axis=0)
    turned = packed.T
    head_real = jnp.where(row >= col, packed, turned)
    head_imag = jnp.where(row < col, packed, jnp.where(row > col, -turned, 0.0))
    head = halves(block_matrix(head_real, -head_imag, head_imag, head_real))
    middle = top(1) + product(head, halves(trans_across))
    right_real = jnp.concatenate([middle[0:LANES], trans_across[0:LANES]], axis=0)
    right_imag = jnp.concatenate([middle[LANES:2 * LANES], trans_across[LANES:2 * LANES]], axis=0)
    for i, value in enumerate((right_real, right_imag, right_real + right_imag)):
        fock_right[0, i], fock_right[1, i] = halves(value)

    loads[6].wait()
    for tile in range(width // TILE):
        cols = pl.ds(tile * TILE, TILE)
        first, second, third = (
            product((fock_left[0, i], fock_left[1, i]), (fock_right[0, i, :, cols], fock_right[1, i, :, cols])) for i in range(3))
        fbuf[0, :, cols] = fbuf[0, :, cols] + (first - second)
        fbuf[1, :, cols] = fbuf[1, :, cols] + ((third - first) - second)
        for part in range(2):
            copy = pltpu.make_async_copy(fbuf.at[part, :, cols], transformed.at[part, :, cols], out_sem.at[1, 2 * tile + part])
            copy.start()
            out_copies.append(copy)

    panel_out.wait()
    for copy in out_copies:
        copy.wait()


def shards(correlation, fock):
    rows, cols = correlation.shape[1:]
    f32, bf16 = jnp.float32, jnp.bfloat16
    hbm, vmem = pl.BlockSpec(memory_space=pl.ANY), pl.BlockSpec(memory_space=pltpu.VMEM)
    dma = pltpu.SemaphoreType.DMA
    rowp, colp, small = pl.pallas_call(
        spread,
        name="spread",
        out_shape=(
            jax.ShapeDtypeStruct((2, 2, rows, LANES), f32),
            jax.ShapeDtypeStruct((2, 2, PANEL, cols), f32),
            jax.ShapeDtypeStruct((2, PANEL, LANES), f32),
        ),
        in_specs=[hbm, hbm],
        out_specs=(hbm, hbm, hbm),
        scratch_shapes=[
            pltpu.VMEM((2, 2, rows, LANES), f32),
            pltpu.VMEM((2, 2, PANEL, cols), f32),
            pltpu.VMEM((2, PANEL, LANES), f32),
            pltpu.VMEM((PANEL, LANES), f32),
            pltpu.VMEM((LANES, LANES), f32),
            pltpu.VMEM((PANEL, LANES), f32),
            pltpu.VMEM((2, PANEL, LANES), f32),
            dma((5,)),
            dma((3,)),
            dma((4, TREE_CHUNKS)),
            dma((4, TREE_CHUNKS)),
            dma((3, CHAIN_CHUNKS)),
            dma((CHAIN_CHUNKS,)),
            dma((2, 12)),
            dma((2,)),
            pltpu.SemaphoreType.REGULAR,
            pltpu.SemaphoreType.REGULAR,
            pltpu.SemaphoreType.REGULAR,
            pltpu.SemaphoreType.REGULAR,
        ],
        compiler_params=pltpu.CompilerParams(collective_id=0, has_side_effects=True),
    )(correlation, fock)
    reduced, transformed, panel = pl.pallas_call(
        update,
        name="update",
        out_shape=(
            jax.ShapeDtypeStruct((2, rows, cols), f32),
            jax.ShapeDtypeStruct((2, rows, cols), f32),
            jax.ShapeDtypeStruct((2, PANEL, rows), f32),
        ),
        in_specs=[hbm, hbm, hbm, hbm, hbm],
        out_specs=(hbm, hbm, hbm),
        scratch_shapes=[
            pltpu.VMEM((2, 2, rows, LANES), f32),
            pltpu.VMEM((2, 2, PANEL, cols), f32),
            pltpu.VMEM((2, PANEL, LANES), f32),
            pltpu.VMEM((2, rows, cols), f32),
            pltpu.VMEM((2, rows, cols), f32),
            pltpu.VMEM((2, PANEL, rows), f32),
            pltpu.VMEM((2, rows, 2 * LANES), bf16),
            pltpu.VMEM((2, 2 * LANES, 2 * cols), bf16),
            pltpu.VMEM((2, 3, rows, 2 * LANES), bf16),
            pltpu.VMEM((2, 3, 2 * LANES, cols), bf16),
            dma((7,)),
            dma((2, 2 * cols // TILE)),
            dma,
        ],
        compiler_params=pltpu.CompilerParams(vmem_limit_bytes=65 * 1000 * 1000),
    )(correlation, fock, rowp, colp, small)
    return reduced, transformed, jnp.swapaxes(panel, 1, 2)


def solution(mesh):
    in_specs = (P(None, "row", "col"), P(None, "row", "col"))
    out_specs = (P(None, "row", "col"), P(None, "row", "col"), P(None, "row", None))
    return jax.shard_map(shards, mesh=mesh, in_specs=in_specs, out_specs=out_specs, check_vma=False)
```

```python
import jax
import jax.numpy as jnp
from jax import lax
from jax.experimental import pallas as pl
from jax.experimental.pallas import tpu as pltpu
from jax.sharding import PartitionSpec as P

PANEL = 96
LANES = 128
MESH = pl.DeviceIdType.MESH

INTO = (-1, 0, 0, 0, 2, 1, 0, 0, 2, 1, 1, 0, 2, 3, 3, 0)
DEPTH = (0, 1, 2, 3, 3, 2, 3, 4, 4, 3, 4, 5, 3, 2, 3, 4)
STEP = ((1, 0), (0, 1), (-1, 0), (0, -1))

TREE_ROWS = 32
TREE_CHUNKS = 2 * LANES // TREE_ROWS
CHAIN_ROWS = 16
CHAIN_CHUNKS = 2 * PANEL // CHAIN_ROWS
TREE_LAG = 5
CHAIN_LAG = 4
CHAIN_START = 0
DOWN_START = 4
STAGE_SLOTS = 5
SMALL_SLOT = 9
EARLY_SLOTS = 5
SLOTS = max(5 * TREE_LAG + TREE_CHUNKS, 4 * CHAIN_LAG + CHAIN_CHUNKS + CHAIN_START + DOWN_START, 4 * STAGE_SLOTS + SMALL_SLOT + EARLY_SLOTS + 1)
GREET_AT = 30
HEAD_AT = 32
HEAD_DOWN_AT = 88
HEAD_LEAD = 4
HEAD_LEAD_DOWN = 1


def rotated(x, y, turns):
    for _ in range(turns % 4):
        x, y = -y % 4, x % 4
    return x, y


def tree_tables():
    depth = [[0] * 16 for _ in range(4)]
    send = [[-1] * 16 for _ in range(4)]
    for tree in range(4):
        for chip in range(16):
            x, y = rotated(chip % 4, chip // 4, -tree)
            depth[tree][chip] = DEPTH[y * 4 + x]
            if chip:
                way = (INTO[y * 4 + x] + tree) % 4
                px, py = (chip % 4 - STEP[way][0]) % 4, (chip // 4 - STEP[way][1]) % 4
                assert send[way][py * 4 + px] == -1
                send[way][py * 4 + px] = tree
    return depth, send


def lookup(index, table):
    value = jnp.int32(0)
    for k, entry in enumerate(table):
        if entry:
            value = value + jnp.where(index == k, jnp.int32(entry), jnp.int32(0))
    return value


def spread(
    corr, fock, rowp_out, colp_out, small_out, rowp, colp, small, wr, wi, dv, head, local_sem, out_sem, tree_send, tree_recv, chain_send, chain_recv, small_send, small_recv, chain_ready, chain_ready_down, small_ready, small_ready_down,
):
    r, c = lax.axis_index("row"), lax.axis_index("col")
    z, core = r // 2, r % 2
    y, x = c // 4, c % 4
    root = (r == 0) & (c == 0)
    depth_table, send_table = tree_tables()

    def along_x(step):
        return (r, 4 * y + (x + step) % 4)

    def along_y(step):
        return (r, 4 * ((y + step) % 4) + x)

    def along_z(step):
        return (2 * ((z + step) % 8) + core, c)

    partner = (r + 1 - 2 * core, c)

    barrier = pltpu.get_barrier_semaphore()
    greeted = [along_x(s) for s in (1, 2, 3)] + [along_y(s) for s in (1, 2, 3)] + [partner]
    for peer in greeted:
        pl.semaphore_signal(barrier, inc=1, device_id=peer, device_id_type=MESH)

    on_chain = core == jnp.where(c == 0, 1, 0)
    edge = (c == 0) & (core == 0)
    chain_up, chain_down = on_chain & (z < 4), on_chain & ((z == 0) | (z > 5))
    z_greetings = (
        (on_chain & (z > 0) & (z < 4), 7), (on_chain & ((z == 5) | (z == 6)), 1),
        (edge & (z == 1), 7), (edge & (z == 2), 6), (edge & (z == 3), 5),
        (on_chain & (z == 3), 1), (on_chain & (z == 0), 7),
        (edge & (z == 3), 1), (edge & (z == 0), 7), (edge & (z == 0), 6), (edge & (z == 6), 7))
    for condition, step in z_greetings:
        @pl.when(condition)
        def _():
            pl.semaphore_signal(barrier, inc=1, device_id=along_z(step), device_id_type=MESH)

    heard = len(greeted) + jnp.where(on_chain & (z != 3) & (z != 5), 1, 0) + jnp.where(on_chain & (z == 7), 1, 0)
    heard = heard + jnp.where(root, 3, 0) + jnp.where(edge & (z > 3), 1, 0)

    def answer():
        pl.semaphore_wait(barrier, heard)

        @pl.when(on_chain & (z == 4))
        def _():
            pl.semaphore_signal(chain_ready, inc=1, device_id=along_z(7), device_id_type=MESH)

        @pl.when(on_chain & (z == 7))
        def _():
            pl.semaphore_signal(chain_ready_down, inc=1, device_id=along_z(1), device_id_type=MESH)

        @pl.when(edge & (z == 4))
        def _():
            pl.semaphore_signal(small_ready, inc=1, device_id=along_z(7), device_id_type=MESH)

        @pl.when(edge & (z > 4))
        def _():
            back = jnp.where(z == 6, 2, 1)
            pl.semaphore_signal(small_ready_down, inc=1, device_id=along_z(back), device_id_type=MESH)

    head_copies = [pltpu.make_async_copy(corr.at[:, pl.ds(0, PANEL), pl.ds(0, LANES)], head, local_sem.at[4])]
    row_copies = [pltpu.make_async_copy(src.at[:, :, pl.ds(0, LANES)], rowp.at[i], local_sem.at[i]) for i, src in enumerate((corr, fock))]
    col_copies = [pltpu.make_async_copy(src.at[:, pl.ds(0, PANEL), :], colp.at[i], local_sem.at[2 + i]) for i, src in enumerate((corr, fock))]

    @pl.when(root)
    def _():
        for copy in head_copies:
            copy.start()

    @pl.when(c == 0)
    def _():
        for copy in row_copies:
            copy.start()

    @pl.when(r == 0)
    def _():
        for copy in col_copies:
            copy.start()

    def loaded():
        @pl.when(c == 0)
        def _():
            for copy in row_copies:
                copy.wait()

        @pl.when(r == 0)
        def _():
            for copy in col_copies:
                copy.wait()

    neighbours = (along_x(1), along_y(1), along_x(3), along_y(3))

    def tree_copy(tree, chunk, way):
        rows = pl.ds(pl.multiple_of(LANES * tree + TREE_ROWS * (chunk % (TREE_CHUNKS // 2)), TREE_ROWS), TREE_ROWS)
        part = rowp.at[chunk // (TREE_CHUNKS // 2), :, rows, :]
        return pltpu.make_async_remote_copy(
            src_ref=part, dst_ref=part, send_sem=tree_send.at[way, chunk], recv_sem=tree_recv.at[tree, chunk],
            device_id=neighbours[way], device_id_type=MESH)

    chain_peers = (along_z(1), along_z(7), partner)

    def chain_copy(chunk, way):
        rows = pl.ds(pl.multiple_of(CHAIN_ROWS * (chunk % (CHAIN_CHUNKS // 2)), CHAIN_ROWS), CHAIN_ROWS)
        part = colp.at[chunk // (CHAIN_CHUNKS // 2), :, rows, :]
        return pltpu.make_async_remote_copy(
            src_ref=part, dst_ref=part, send_sem=chain_send.at[way, chunk], recv_sem=chain_recv.at[chunk],
            device_id=chain_peers[way], device_id_type=MESH)

    def small_copy(which, index, peer):
        return pltpu.make_async_remote_copy(
            src_ref=small.at[which], dst_ref=small.at[which], send_sem=small_send.at[which, index],
            recv_sem=small_recv.at[which], device_id=peer, device_id_type=MESH)

    def small_groups(which):
        z_steps = [small_copy(which, i, along_z(s)) for i, s in enumerate((3, 6, 2, 7, 1))]
        x_steps = [small_copy(which, 5 + i, along_x(s)) for i, s in enumerate((2, 1, 3))]
        y_steps = [small_copy(which, 8 + i, along_y(s)) for i, s in enumerate((2, 1, 3))]
        return (
            (root, [z_steps[0], z_steps[2], z_steps[4]]), (edge & (z == 3), [z_steps[4]]), (edge & (z == 6), [z_steps[3]]),
            (edge, x_steps), ((y == 0) & (core == 0), y_steps), (core == 0, [small_copy(which, 11, partner)]),
            (root, [z_steps[1], z_steps[3]]))

    def small_forward(which):
        for condition, copies in small_groups(which)[:-1]:
            @pl.when(condition)
            def _():
                for copy in copies:
                    copy.start()

    def small_event(which):
        small_copy(which, 11, partner).wait_recv()
        small_forward(which)

    send_tree = [lookup(c, [entry + 1 for entry in send_table[way]]) - 1 for way in range(4)]
    chain_ways = (chain_up, chain_down, root | (on_chain & jnp.logical_not((r == 1) & (c == 0))))

    @pl.when(root)
    def _():
        lane = lax.broadcasted_iota(jnp.int32, (PANEL, LANES), 1)
        row = lax.broadcasted_iota(jnp.int32, (PANEL, LANES), 0)
        inside = lane < PANEL
        for copy in head_copies:
            copy.wait()

        tile_lane = lax.broadcasted_iota(jnp.int32, (8, LANES), 1)
        tile_row = lax.broadcasted_iota(jnp.int32, (8, LANES), 0)
        count = PANEL // 8
        real = [head[0, pl.ds(8 * t, 8), :] for t in range(count)]
        imag = [head[1, pl.ds(8 * t, 8), :] for t in range(count)]

        def down(value, j):
            return jnp.broadcast_to(value[j:j + 1, :], (8, LANES))

        def across(value, j):
            return jnp.broadcast_to(value[:, j:j + 1], (8, LANES))

        for k in range(0, PANEL, 2):
            tile, j = k // 8, k % 8
            first, second = tile_lane == k, tile_lane == k + 1
            col_a = [(across(real[t], k), across(imag[t], k)) for t in range(tile, count)]
            col_b = [(across(real[t], k + 1), across(imag[t], k + 1)) for t in range(tile, count)]
            pivot_a = down(col_a[0][0], j)
            off_real, off_imag = down(col_a[0][0], j + 1), down(col_a[0][1], j + 1)
            inv_a = 1.0 / pivot_a
            low_real, low_imag = off_real * inv_a, off_imag * inv_a
            pivot_b = down(col_b[0][0], j + 1) - (off_real * low_real + off_imag * low_imag)
            inv_b = 1.0 / pivot_b
            both = first | second
            a_real = jnp.where(both, jnp.where(first, 1.0, 0.0), down(real[tile], j))
            a_imag = jnp.where(both, 0.0, down(imag[tile], j))
            b_real = jnp.where(both, jnp.where(second, 1.0, 0.0), down(real[tile], j + 1))
            b_imag = jnp.where(both, 0.0, down(imag[tile], j + 1))
            b_real, b_imag = (
                b_real - (low_real * a_real - low_imag * a_imag), b_imag - (low_real * a_imag + low_imag * a_real))
            wb_real, wb_imag = b_real * inv_b, b_imag * inv_b
            wa_real = a_real * inv_a - (low_real * wb_real + low_imag * wb_imag)
            wa_imag = a_imag * inv_a - (low_real * wb_imag - low_imag * wb_real)
            for t in range(tile, count):
                (ar, ai), (br, bi) = col_a[t - tile], col_b[t - tile]
                next_real = jnp.where(both, 0.0, real[t]) - ((ar * wa_real - ai * wa_imag) + (br * wb_real - bi * wb_imag))
                next_imag = jnp.where(both, 0.0, imag[t]) - ((ar * wa_imag + ai * wa_real) + (br * wb_imag + bi * wb_real))
                if t == tile:
                    keep = tile_row < j
                    next_real = jnp.where(keep, real[t], jnp.where(tile_row == j, a_real, jnp.where(tile_row == j + 1, b_real, next_real)))
                    next_imag = jnp.where(keep, imag[t], jnp.where(tile_row == j, a_imag, jnp.where(tile_row == j + 1, b_imag, next_imag)))
                real[t], imag[t] = next_real, next_imag
            dv[pl.ds(k, 1), :] = pivot_a[0:1, :]
            dv[pl.ds(k + 1, 1), :] = pivot_b[0:1, :]

            if k == GREET_AT:
                loaded()
                answer()
                for chunk in range(TREE_CHUNKS):
                    for way in range(4):
                        tree_copy(way, chunk, way).start()
                for chunk in range(CHAIN_CHUNKS):
                    chain_copy(chunk, 2).start()

            if k == HEAD_AT:
                head_real = rowp[1, 0, pl.ds(0, PANEL), :]
                head_imag = rowp[1, 1, pl.ds(0, PANEL), :]
                small[0] = jnp.where(inside, jnp.where(lane <= row, head_real, head_imag), 0.0)
                small_forward(0)

            if k == HEAD_DOWN_AT:
                pl.semaphore_wait(small_ready_down, 2)
                for copy in small_groups(0)[-1][1]:
                    copy.start()

        pivots = dv[...]
        scale = lax.rsqrt(pivots)
        scale = scale * (1.5 - 0.5 * pivots * scale * scale)
        for t in range(count):
            lower = tile_lane <= tile_row + 8 * t
            rows = pl.ds(8 * t, 8)
            wr[rows, :] = jnp.where(lower, real[t], 0.0)
            wi[rows, :] = jnp.where(lower, imag[t], 0.0)
        wi[pl.ds(0, PANEL), :] = wi[pl.ds(0, PANEL), :] * scale
        wi[pl.ds(PANEL, LANES - PANEL), :] = jnp.zeros((LANES - PANEL, LANES), jnp.float32)
        small[1] = wr[...] * scale + wi[...].T[0:PANEL, :]
        small_forward(1)
        for copy in small_groups(1)[-1][1]:
            copy.start()

    @pl.when(jnp.logical_not(root))
    def _():
        loaded()
        answer()
        depth = [lookup(c, depth_table[tree]) for tree in range(4)]
        way_start = [
            jnp.where((c == 0) | (send_tree[way] < 0), SLOTS, TREE_LAG * lookup(c, [
                depth_table[tree][chip] if tree >= 0 else 0 for chip, tree in enumerate(send_table[way])]))
            for way in range(4)]
        chain_depth = jnp.where(z <= 4, z, 8 - z)
        chain_now = (chain_up, on_chain & (z > 5), chain_ways[2])
        chain_depth_slots = CHAIN_LAG * chain_depth + CHAIN_START + jnp.where(z > 4, DOWN_START, 0)
        stage = jnp.where(z == 0, 0, jnp.where((z == 4) | (z == 5), 2, 1)) + jnp.where(x == 0, 0, 1) + jnp.where(y == 0, 0, 1)
        middle = (z > 0) & (z < 5)
        small_slot = SMALL_SLOT + STAGE_SLOTS * stage + jnp.where(z < 4, EARLY_SLOTS, 0) - jnp.where(middle, stage + 1, 0)
        head_slot = small_slot - jnp.where(z < 5, HEAD_LEAD, HEAD_LEAD_DOWN)

        @pl.when(c == 0)
        def _():
            def source(chunk, carry):
                for way in range(4):
                    tree_copy(way, chunk, way).start()
                return carry

            lax.fori_loop(0, TREE_CHUNKS, source, 0)

        def slot(s, carry):
            for tree in range(4):
                chunk = s - TREE_LAG * depth[tree]

                @pl.when((c != 0) & (chunk >= 0) & (chunk < TREE_CHUNKS))
                def _():
                    tree_copy(tree, chunk, 0).wait_recv()

            for way in range(4):
                onward = s - way_start[way]

                @pl.when((onward >= 0) & (onward < TREE_CHUNKS))
                def _():
                    tree_copy(send_tree[way], onward, way).start()

            link = s - chain_depth_slots

            @pl.when(on_chain & (link >= 0) & (link < CHAIN_CHUNKS))
            def _():
                @pl.when((z != 0) | (c == 0))
                def _():
                    chain_copy(link, 0).wait_recv()

                @pl.when((link == 0) & (z == 3))
                def _():
                    pl.semaphore_wait(chain_ready, 1)

                for way in range(3):
                    @pl.when(chain_now[way])
                    def _():
                        chain_copy(link, way).start()

            link_down = s - CHAIN_START - DOWN_START

            @pl.when(on_chain & (z == 0) & (link_down >= 0) & (link_down < CHAIN_CHUNKS))
            def _():
                @pl.when(link_down == 0)
                def _():
                    pl.semaphore_wait(chain_ready_down, 1)

                chain_copy(link_down, 1).start()

            @pl.when(s == head_slot)
            def _():
                @pl.when(edge & (z == 3))
                def _():
                    pl.semaphore_wait(small_ready, 1)

                @pl.when(edge & (z == 6))
                def _():
                    pl.semaphore_wait(small_ready_down, 1)

                small_event(0)

            @pl.when(s == small_slot)
            def _():
                small_event(1)

            return carry

        lax.fori_loop(0, SLOTS, slot, 0)

        @pl.when(jnp.logical_not(on_chain))
        def _():
            def arrived(chunk, carry):
                chain_copy(chunk, 2).wait_recv()
                return carry

            lax.fori_loop(0, CHAIN_CHUNKS, arrived, 0)

    flushes = [
        pltpu.make_async_copy(src, dst, out_sem.at[i])
        for i, (src, dst) in enumerate(((small, small_out), (rowp, rowp_out), (colp, colp_out)))]
    for flush in flushes:
        flush.start()

    for way in range(4):
        @pl.when(send_tree[way] >= 0)
        def _():
            def sent(chunk, carry):
                tree_copy(0, chunk, way).wait_send()
                return carry

            lax.fori_loop(0, TREE_CHUNKS, sent, 0)

    for way in range(3):
        @pl.when(chain_ways[way])
        def _():
            def sent(chunk, carry):
                chain_copy(chunk, way).wait_send()
                return carry

            lax.fori_loop(0, CHAIN_CHUNKS, sent, 0)

    for which in range(2):
        for condition, copies in small_groups(which):
            @pl.when(condition)
            def _():
                for copy in copies:
                    copy.wait_send()

    for flush in flushes:
        flush.wait()


def halves(value):
    high = value.astype(jnp.bfloat16)
    return high, (value - high.astype(jnp.float32)).astype(jnp.bfloat16)


def product(left, right):
    (left_high, left_low), (right_high, right_low) = left, right

    def dot(a, b):
        return jnp.dot(a, b, preferred_element_type=jnp.float32)

    return dot(left_high, right_high) + (dot(left_low, right_high) + dot(left_high, right_low))


def block_matrix(a, b, c, d):
    return jnp.concatenate([jnp.concatenate([a, b], axis=1), jnp.concatenate([c, d], axis=1)], axis=0)


TILE = 256


def update(
    corr, fock, rowp_in, colp_in, small_in, over, transformed, panel, rowp, colp, small, cbuf, fbuf, pbuf,
    over_left, over_right, fock_left, fock_right, in_sem, out_sem, panel_sem,
):
    r, c = lax.axis_index("row"), lax.axis_index("col")
    pairs = (
        (small_in, small), (rowp_in.at[0], rowp.at[0]), (colp_in.at[0], colp.at[0]), (corr, cbuf),
        (rowp_in.at[1], rowp.at[1]), (colp_in.at[1], colp.at[1]), (fock, fbuf))
    loads = [pltpu.make_async_copy(src, dst, in_sem.at[i]) for i, (src, dst) in enumerate(pairs)]
    for load in loads:
        load.start()
    loads[0].wait()

    size = rowp.shape[2]
    width = colp.shape[3]
    row = lax.broadcasted_iota(jnp.int32, (LANES, LANES), 0)
    col = lax.broadcasted_iota(jnp.int32, (LANES, LANES), 1)
    rest = jnp.zeros((LANES - PANEL, LANES), jnp.float32)
    packed = jnp.concatenate([small[1], rest], axis=0)
    turned = packed.T
    inv_real = jnp.where(row >= col, packed, 0.0)
    inv_imag = jnp.where(row > col, turned, 0.0)
    inv_real_t = jnp.where(row <= col, turned, 0.0)
    inv_imag_t = jnp.where(row < col, packed, 0.0)
    right_adjoint = halves(block_matrix(inv_real_t, -inv_imag_t, inv_imag_t, inv_real_t))
    right_inverse = halves(block_matrix(inv_real, inv_imag, -inv_imag, inv_real))
    left_inverse = halves(block_matrix(inv_real, -inv_imag, inv_imag, inv_real))
    left_adjoint = halves(block_matrix(inv_real_t, inv_imag_t, -inv_imag_t, inv_real_t))

    gap = jnp.zeros((LANES - PANEL, width), jnp.float32)

    def top(which):
        return jnp.concatenate([colp[which, 0], gap, colp[which, 1], gap], axis=0)

    loads[1].wait()
    factor = product(halves(jnp.concatenate([rowp[0, 0], rowp[0, 1]], axis=1)), right_adjoint)
    pbuf[0] = factor[:, 0:LANES].T[0:PANEL]
    pbuf[1] = factor[:, LANES:2 * LANES].T[0:PANEL]
    panel_out = pltpu.make_async_copy(pbuf, panel, panel_sem)
    panel_out.start()
    over_left[0], over_left[1] = halves(factor)
    loads[2].wait()
    across = product(left_inverse, halves(top(0)))

    def right_side(value):
        real, imag = value[0:LANES], value[LANES:2 * LANES]
        return block_matrix(real, imag, -imag, real)

    over_right[0], over_right[1] = halves(right_side(across))

    out_copies = []

    def outer_tiles(left, right, buffer, target, which, sign):
        for tile in range(2 * width // TILE):
            part, cols = tile // (width // TILE), pl.ds(tile % (width // TILE) * TILE, TILE)
            columns = pl.ds(tile * TILE, TILE)
            piece = product((left[0], left[1]), (right[0, :, columns], right[1, :, columns]))
            old = buffer[part, :, cols]
            buffer[part, :, cols] = old + piece if sign > 0 else old - piece
            copy = pltpu.make_async_copy(buffer.at[part, :, cols], target.at[part, :, cols], out_sem.at[which, tile])
            copy.start()
            out_copies.append(copy)

    loads[3].wait()
    outer_tiles(over_left, over_right, cbuf, over, 0, -1)

    wide_row = lax.broadcasted_iota(jnp.int32, (size, 2 * LANES), 0) + r * size
    wide_lane = lax.broadcasted_iota(jnp.int32, (size, 2 * LANES), 1)
    unit = jnp.where((wide_row == wide_lane) & (wide_lane < PANEL), 1.0, 0.0)
    trans = product(halves(unit - factor), right_inverse)
    loads[4].wait()
    loads[5].wait()
    left_real = jnp.concatenate([trans[:, 0:LANES], rowp[1, 0]], axis=1)
    left_imag = jnp.concatenate([trans[:, LANES:2 * LANES], rowp[1, 1]], axis=1)
    for i, value in enumerate((left_real, left_imag, left_real + left_imag)):
        fock_left[0, i], fock_left[1, i] = halves(value)
    tall_row = lax.broadcasted_iota(jnp.int32, (2 * LANES, width), 0)
    tall_lane = lax.broadcasted_iota(jnp.int32, (2 * LANES, width), 1) + c * width
    unit = jnp.where((tall_row == tall_lane) & (tall_row < PANEL), 1.0, 0.0)
    trans_across = product(left_adjoint, halves(unit - across))

    packed = jnp.concatenate([small[0], rest], axis=0)
    turned = packed.T
    head_real = jnp.where(row >= col, packed, turned)
    head_imag = jnp.where(row < col, packed, jnp.where(row > col, -turned, 0.0))
    head = halves(block_matrix(head_real, -head_imag, head_imag, head_real))
    middle = top(1) + product(head, halves(trans_across))
    right_real = jnp.concatenate([middle[0:LANES], trans_across[0:LANES]], axis=0)
    right_imag = jnp.concatenate([middle[LANES:2 * LANES], trans_across[LANES:2 * LANES]], axis=0)
    for i, value in enumerate((right_real, right_imag, right_real + right_imag)):
        fock_right[0, i], fock_right[1, i] = halves(value)

    loads[6].wait()
    for tile in range(width // TILE):
        cols = pl.ds(tile * TILE, TILE)
        first, second, third = (
            product((fock_left[0, i], fock_left[1, i]), (fock_right[0, i, :, cols], fock_right[1, i, :, cols])) for i in range(3))
        fbuf[0, :, cols] = fbuf[0, :, cols] + (first - second)
        fbuf[1, :, cols] = fbuf[1, :, cols] + ((third - first) - second)
        for part in range(2):
            copy = pltpu.make_async_copy(fbuf.at[part, :, cols], transformed.at[part, :, cols], out_sem.at[1, 2 * tile + part])
            copy.start()
            out_copies.append(copy)

    panel_out.wait()
    for copy in out_copies:
        copy.wait()


def shards(correlation, fock):
    rows, cols = correlation.shape[1:]
    f32, bf16 = jnp.float32, jnp.bfloat16
    hbm, vmem = pl.BlockSpec(memory_space=pl.ANY), pl.BlockSpec(memory_space=pltpu.VMEM)
    dma = pltpu.SemaphoreType.DMA
    rowp, colp, small = pl.pallas_call(
        spread,
        name="spread",
        out_shape=(
            jax.ShapeDtypeStruct((2, 2, rows, LANES), f32),
            jax.ShapeDtypeStruct((2, 2, PANEL, cols), f32),
            jax.ShapeDtypeStruct((2, PANEL, LANES), f32),
        ),
        in_specs=[hbm, hbm],
        out_specs=(hbm, hbm, hbm),
        scratch_shapes=[
            pltpu.VMEM((2, 2, rows, LANES), f32),
            pltpu.VMEM((2, 2, PANEL, cols), f32),
            pltpu.VMEM((2, PANEL, LANES), f32),
            pltpu.VMEM((PANEL, LANES), f32),
            pltpu.VMEM((LANES, LANES), f32),
            pltpu.VMEM((PANEL, LANES), f32),
            pltpu.VMEM((2, PANEL, LANES), f32),
            dma((5,)),
            dma((3,)),
            dma((4, TREE_CHUNKS)),
            dma((4, TREE_CHUNKS)),
            dma((3, CHAIN_CHUNKS)),
            dma((CHAIN_CHUNKS,)),
            dma((2, 12)),
            dma((2,)),
            pltpu.SemaphoreType.REGULAR,
            pltpu.SemaphoreType.REGULAR,
            pltpu.SemaphoreType.REGULAR,
            pltpu.SemaphoreType.REGULAR,
        ],
        compiler_params=pltpu.CompilerParams(collective_id=0, has_side_effects=True),
    )(correlation, fock)
    reduced, transformed, panel = pl.pallas_call(
        update,
        name="update",
        out_shape=(
            jax.ShapeDtypeStruct((2, rows, cols), f32),
            jax.ShapeDtypeStruct((2, rows, cols), f32),
            jax.ShapeDtypeStruct((2, PANEL, rows), f32),
        ),
        in_specs=[hbm, hbm, hbm, hbm, hbm],
        out_specs=(hbm, hbm, hbm),
        scratch_shapes=[
            pltpu.VMEM((2, 2, rows, LANES), f32),
            pltpu.VMEM((2, 2, PANEL, cols), f32),
            pltpu.VMEM((2, PANEL, LANES), f32),
            pltpu.VMEM((2, rows, cols), f32),
            pltpu.VMEM((2, rows, cols), f32),
            pltpu.VMEM((2, PANEL, rows), f32),
            pltpu.VMEM((2, rows, 2 * LANES), bf16),
            pltpu.VMEM((2, 2 * LANES, 2 * cols), bf16),
            pltpu.VMEM((2, 3, rows, 2 * LANES), bf16),
            pltpu.VMEM((2, 3, 2 * LANES, cols), bf16),
            dma((7,)),
            dma((2, 2 * cols // TILE)),
            dma,
        ],
        compiler_params=pltpu.CompilerParams(vmem_limit_bytes=65 * 1000 * 1000),
    )(correlation, fock, rowp, colp, small)
    return reduced, transformed, jnp.swapaxes(panel, 1, 2)


def solution(mesh):
    in_specs = (P(None, "row", "col"), P(None, "row", "col"))
    out_specs = (P(None, "row", "col"), P(None, "row", "col"), P(None, "row", None))
    return jax.shard_map(shards, mesh=mesh, in_specs=in_specs, out_specs=out_specs, check_vma=False)
```

```python
import jax
import jax.numpy as jnp
from jax import lax
from jax.experimental import pallas as pl
from jax.experimental.pallas import tpu as pltpu
from jax.sharding import PartitionSpec as P

PANEL = 96
LANES = 128
MESH = pl.DeviceIdType.MESH

INTO = (-1, 0, 0, 0, 2, 1, 0, 0, 2, 1, 1, 0, 2, 3, 3, 0)
DEPTH = (0, 1, 2, 3, 3, 2, 3, 4, 4, 3, 4, 5, 3, 2, 3, 4)
STEP = ((1, 0), (0, 1), (-1, 0), (0, -1))

TREE_ROWS = 32
TREE_CHUNKS = 2 * LANES // TREE_ROWS
CHAIN_ROWS = 16
CHAIN_CHUNKS = 2 * PANEL // CHAIN_ROWS
TREE_LAG = 5
CHAIN_LAG = 4
CHAIN_START = 0
DOWN_START = 4
STAGE_SLOTS = 5
SMALL_SLOT = 9
EARLY_SLOTS = 5
SLOTS = max(5 * TREE_LAG + TREE_CHUNKS, 4 * CHAIN_LAG + CHAIN_CHUNKS + CHAIN_START + DOWN_START, 4 * STAGE_SLOTS + SMALL_SLOT + EARLY_SLOTS + 1)
GREET_AT = 30
HEAD_AT = 32
HEAD_DOWN_AT = 88
HEAD_LEAD = 4
HEAD_LEAD_DOWN = 1


def rotated(x, y, turns):
    for _ in range(turns % 4):
        x, y = -y % 4, x % 4
    return x, y


def tree_tables():
    depth = [[0] * 16 for _ in range(4)]
    send = [[-1] * 16 for _ in range(4)]
    for tree in range(4):
        for chip in range(16):
            x, y = rotated(chip % 4, chip // 4, -tree)
            depth[tree][chip] = DEPTH[y * 4 + x]
            if chip:
                way = (INTO[y * 4 + x] + tree) % 4
                px, py = (chip % 4 - STEP[way][0]) % 4, (chip // 4 - STEP[way][1]) % 4
                assert send[way][py * 4 + px] == -1
                send[way][py * 4 + px] = tree
    return depth, send


def lookup(index, table):
    value = jnp.int32(0)
    for k, entry in enumerate(table):
        if entry:
            value = value + jnp.where(index == k, jnp.int32(entry), jnp.int32(0))
    return value


def spread(
    corr, fock, rowp_out, colp_out, small_out, rowp, colp, small, wr, wi, dv, head, local_sem, out_sem, tree_send, tree_recv, chain_send, chain_recv, small_send, small_recv, chain_ready, chain_ready_down, small_ready, small_ready_down,
):
    r, c = lax.axis_index("row"), lax.axis_index("col")
    z, core = r // 2, r % 2
    y, x = c // 4, c % 4
    root = (r == 0) & (c == 0)
    depth_table, send_table = tree_tables()

    def along_x(step):
        return (r, 4 * y + (x + step) % 4)

    def along_y(step):
        return (r, 4 * ((y + step) % 4) + x)

    def along_z(step):
        return (2 * ((z + step) % 8) + core, c)

    partner = (r + 1 - 2 * core, c)

    barrier = pltpu.get_barrier_semaphore()
    greeted = [along_x(s) for s in (1, 2, 3)] + [along_y(s) for s in (1, 2, 3)] + [partner]
    for peer in greeted:
        pl.semaphore_signal(barrier, inc=1, device_id=peer, device_id_type=MESH)

    on_chain = core == jnp.where(c == 0, 1, 0)
    edge = (c == 0) & (core == 0)
    chain_up, chain_down = on_chain & (z < 4), on_chain & ((z == 0) | (z > 5))
    z_greetings = (
        (on_chain & (z > 0) & (z < 4), 7), (on_chain & ((z == 5) | (z == 6)), 1),
        (edge & (z == 1), 7), (edge & (z == 2), 6), (edge & (z == 3), 5),
        (on_chain & (z == 3), 1), (on_chain & (z == 0), 7),
        (edge & (z == 3), 1), (edge & (z == 0), 7), (edge & (z == 0), 6), (edge & (z == 6), 7))
    for condition, step in z_greetings:
        @pl.when(condition)
        def _():
            pl.semaphore_signal(barrier, inc=1, device_id=along_z(step), device_id_type=MESH)

    heard = len(greeted) + jnp.where(on_chain & (z != 3) & (z != 5), 1, 0) + jnp.where(on_chain & (z == 7), 1, 0)
    heard = heard + jnp.where(root, 3, 0) + jnp.where(edge & (z > 3), 1, 0)

    def answer():
        pl.semaphore_wait(barrier, heard)

        @pl.when(on_chain & (z == 4))
        def _():
            pl.semaphore_signal(chain_ready, inc=1, device_id=along_z(7), device_id_type=MESH)

        @pl.when(on_chain & (z == 7))
        def _():
            pl.semaphore_signal(chain_ready_down, inc=1, device_id=along_z(1), device_id_type=MESH)

        @pl.when(edge & (z == 4))
        def _():
            pl.semaphore_signal(small_ready, inc=1, device_id=along_z(7), device_id_type=MESH)

        @pl.when(edge & (z > 4))
        def _():
            back = jnp.where(z == 6, 2, 1)
            pl.semaphore_signal(small_ready_down, inc=1, device_id=along_z(back), device_id_type=MESH)

    head_copies = [pltpu.make_async_copy(corr.at[:, pl.ds(0, PANEL), pl.ds(0, LANES)], head, local_sem.at[4])]
    row_copies = [pltpu.make_async_copy(src.at[:, :, pl.ds(0, LANES)], rowp.at[i], local_sem.at[i]) for i, src in enumerate((corr, fock))]
    col_copies = [pltpu.make_async_copy(src.at[:, pl.ds(0, PANEL), :], colp.at[i], local_sem.at[2 + i]) for i, src in enumerate((corr, fock))]

    @pl.when(root)
    def _():
        for copy in head_copies:
            copy.start()

    @pl.when(c == 0)
    def _():
        for copy in row_copies:
            copy.start()

    @pl.when(r == 0)
    def _():
        for copy in col_copies:
            copy.start()

    def loaded():
        @pl.when(c == 0)
        def _():
            for copy in row_copies:
                copy.wait()

        @pl.when(r == 0)
        def _():
            for copy in col_copies:
                copy.wait()

    neighbours = (along_x(1), along_y(1), along_x(3), along_y(3))

    def tree_copy(tree, chunk, way):
        rows = pl.ds(pl.multiple_of(LANES * tree + TREE_ROWS * (chunk % (TREE_CHUNKS // 2)), TREE_ROWS), TREE_ROWS)
        part = rowp.at[chunk // (TREE_CHUNKS // 2), :, rows, :]
        return pltpu.make_async_remote_copy(
            src_ref=part, dst_ref=part, send_sem=tree_send.at[way, chunk], recv_sem=tree_recv.at[tree, chunk],
            device_id=neighbours[way], device_id_type=MESH)

    chain_peers = (along_z(1), along_z(7), partner)

    def chain_copy(chunk, way):
        rows = pl.ds(pl.multiple_of(CHAIN_ROWS * (chunk % (CHAIN_CHUNKS // 2)), CHAIN_ROWS), CHAIN_ROWS)
        part = colp.at[chunk // (CHAIN_CHUNKS // 2), :, rows, :]
        return pltpu.make_async_remote_copy(
            src_ref=part, dst_ref=part, send_sem=chain_send.at[way, chunk], recv_sem=chain_recv.at[chunk],
            device_id=chain_peers[way], device_id_type=MESH)

    def small_copy(which, index, peer):
        return pltpu.make_async_remote_copy(
            src_ref=small.at[which], dst_ref=small.at[which], send_sem=small_send.at[which, index],
            recv_sem=small_recv.at[which], device_id=peer, device_id_type=MESH)

    def small_groups(which):
        z_steps = [small_copy(which, i, along_z(s)) for i, s in enumerate((3, 6, 2, 7, 1))]
        x_steps = [small_copy(which, 5 + i, along_x(s)) for i, s in enumerate((2, 1, 3))]
        y_steps = [small_copy(which, 8 + i, along_y(s)) for i, s in enumerate((2, 1, 3))]
        return (
            (root, [z_steps[0], z_steps[2], z_steps[4]]), (edge & (z == 3), [z_steps[4]]), (edge & (z == 6), [z_steps[3]]),
            (edge, x_steps), ((y == 0) & (core == 0), y_steps), (core == 0, [small_copy(which, 11, partner)]),
            (root, [z_steps[1], z_steps[3]]))

    def small_forward(which):
        for condition, copies in small_groups(which)[:-1]:
            @pl.when(condition)
            def _():
                for copy in copies:
                    copy.start()

    def small_event(which):
        small_copy(which, 11, partner).wait_recv()
        small_forward(which)

    send_tree = [lookup(c, [entry + 1 for entry in send_table[way]]) - 1 for way in range(4)]
    chain_ways = (chain_up, chain_down, root | (on_chain & jnp.logical_not((r == 1) & (c == 0))))

    first_flush = pltpu.make_async_copy(rowp.at[0], rowp_out.at[0], out_sem.at[3])
    flush_slot = 5 * TREE_LAG + TREE_CHUNKS // 2

    @pl.when(root)
    def _():
        lane = lax.broadcasted_iota(jnp.int32, (PANEL, LANES), 1)
        row = lax.broadcasted_iota(jnp.int32, (PANEL, LANES), 0)
        inside = lane < PANEL
        for copy in head_copies:
            copy.wait()

        tile_lane = lax.broadcasted_iota(jnp.int32, (8, LANES), 1)
        tile_row = lax.broadcasted_iota(jnp.int32, (8, LANES), 0)
        count = PANEL // 8
        real = [head[0, pl.ds(8 * t, 8), :] for t in range(count)]
        imag = [head[1, pl.ds(8 * t, 8), :] for t in range(count)]

        def down(value, j):
            return jnp.broadcast_to(value[j:j + 1, :], (8, LANES))

        def across(value, j):
            return jnp.broadcast_to(value[:, j:j + 1], (8, LANES))

        for k in range(0, PANEL, 2):
            tile, j = k // 8, k % 8
            first, second = tile_lane == k, tile_lane == k + 1
            col_a = [(across(real[t], k), across(imag[t], k)) for t in range(tile, count)]
            col_b = [(across(real[t], k + 1), across(imag[t], k + 1)) for t in range(tile, count)]
            pivot_a = down(col_a[0][0], j)
            off_real, off_imag = down(col_a[0][0], j + 1), down(col_a[0][1], j + 1)
            inv_a = 1.0 / pivot_a
            low_real, low_imag = off_real * inv_a, off_imag * inv_a
            pivot_b = down(col_b[0][0], j + 1) - (off_real * low_real + off_imag * low_imag)
            inv_b = 1.0 / pivot_b
            both = first | second
            a_real = jnp.where(both, jnp.where(first, 1.0, 0.0), down(real[tile], j))
            a_imag = jnp.where(both, 0.0, down(imag[tile], j))
            b_real = jnp.where(both, jnp.where(second, 1.0, 0.0), down(real[tile], j + 1))
            b_imag = jnp.where(both, 0.0, down(imag[tile], j + 1))
            b_real, b_imag = (
                b_real - (low_real * a_real - low_imag * a_imag), b_imag - (low_real * a_imag + low_imag * a_real))
            wb_real, wb_imag = b_real * inv_b, b_imag * inv_b
            wa_real = a_real * inv_a - (low_real * wb_real + low_imag * wb_imag)
            wa_imag = a_imag * inv_a - (low_real * wb_imag - low_imag * wb_real)
            for t in range(tile, count):
                (ar, ai), (br, bi) = col_a[t - tile], col_b[t - tile]
                next_real = jnp.where(both, 0.0, real[t]) - ((ar * wa_real - ai * wa_imag) + (br * wb_real - bi * wb_imag))
                next_imag = jnp.where(both, 0.0, imag[t]) - ((ar * wa_imag + ai * wa_real) + (br * wb_imag + bi * wb_real))
                if t == tile:
                    keep = tile_row < j
                    next_real = jnp.where(keep, real[t], jnp.where(tile_row == j, a_real, jnp.where(tile_row == j + 1, b_real, next_real)))
                    next_imag = jnp.where(keep, imag[t], jnp.where(tile_row == j, a_imag, jnp.where(tile_row == j + 1, b_imag, next_imag)))
                real[t], imag[t] = next_real, next_imag
            dv[pl.ds(k, 1), :] = pivot_a[0:1, :]
            dv[pl.ds(k + 1, 1), :] = pivot_b[0:1, :]

            if k == GREET_AT:
                loaded()
                answer()
                for chunk in range(TREE_CHUNKS):
                    for way in range(4):
                        tree_copy(way, chunk, way).start()
                for chunk in range(CHAIN_CHUNKS):
                    chain_copy(chunk, 2).start()

            if k == HEAD_AT:
                head_real = rowp[1, 0, pl.ds(0, PANEL), :]
                head_imag = rowp[1, 1, pl.ds(0, PANEL), :]
                small[0] = jnp.where(inside, jnp.where(lane <= row, head_real, head_imag), 0.0)
                small_forward(0)

            if k == HEAD_DOWN_AT:
                pl.semaphore_wait(small_ready_down, 2)
                for copy in small_groups(0)[-1][1]:
                    copy.start()

        pivots = dv[...]
        scale = lax.rsqrt(pivots)
        scale = scale * (1.5 - 0.5 * pivots * scale * scale)
        for t in range(count):
            lower = tile_lane <= tile_row + 8 * t
            rows = pl.ds(8 * t, 8)
            wr[rows, :] = jnp.where(lower, real[t], 0.0)
            wi[rows, :] = jnp.where(lower, imag[t], 0.0)
        wi[pl.ds(0, PANEL), :] = wi[pl.ds(0, PANEL), :] * scale
        wi[pl.ds(PANEL, LANES - PANEL), :] = jnp.zeros((LANES - PANEL, LANES), jnp.float32)
        small[1] = wr[...] * scale + wi[...].T[0:PANEL, :]
        small_forward(1)
        for copy in small_groups(1)[-1][1]:
            copy.start()
        first_flush.start()

    @pl.when(jnp.logical_not(root))
    def _():
        loaded()
        answer()
        depth = [lookup(c, depth_table[tree]) for tree in range(4)]
        way_start = [
            jnp.where((c == 0) | (send_tree[way] < 0), SLOTS, TREE_LAG * lookup(c, [
                depth_table[tree][chip] if tree >= 0 else 0 for chip, tree in enumerate(send_table[way])]))
            for way in range(4)]
        chain_depth = jnp.where(z <= 4, z, 8 - z)
        chain_now = (chain_up, on_chain & (z > 5), chain_ways[2])
        chain_depth_slots = CHAIN_LAG * chain_depth + CHAIN_START + jnp.where(z > 4, DOWN_START, 0)
        stage = jnp.where(z == 0, 0, jnp.where((z == 4) | (z == 5), 2, 1)) + jnp.where(x == 0, 0, 1) + jnp.where(y == 0, 0, 1)
        middle = (z > 0) & (z < 5)
        small_slot = SMALL_SLOT + STAGE_SLOTS * stage + jnp.where(z < 4, EARLY_SLOTS, 0) - jnp.where(middle, stage + 1, 0)
        head_slot = small_slot - jnp.where(z < 5, HEAD_LEAD, HEAD_LEAD_DOWN)

        @pl.when(c == 0)
        def _():
            def source(chunk, carry):
                for way in range(4):
                    tree_copy(way, chunk, way).start()
                return carry

            lax.fori_loop(0, TREE_CHUNKS, source, 0)

        def slot(s, carry):
            for tree in range(4):
                chunk = s - TREE_LAG * depth[tree]

                @pl.when((c != 0) & (chunk >= 0) & (chunk < TREE_CHUNKS))
                def _():
                    tree_copy(tree, chunk, 0).wait_recv()

            for way in range(4):
                onward = s - way_start[way]

                @pl.when((onward >= 0) & (onward < TREE_CHUNKS))
                def _():
                    tree_copy(send_tree[way], onward, way).start()

            link = s - chain_depth_slots

            @pl.when(on_chain & (link >= 0) & (link < CHAIN_CHUNKS))
            def _():
                @pl.when((z != 0) | (c == 0))
                def _():
                    chain_copy(link, 0).wait_recv()

                @pl.when((link == 0) & (z == 3))
                def _():
                    pl.semaphore_wait(chain_ready, 1)

                for way in range(3):
                    @pl.when(chain_now[way])
                    def _():
                        chain_copy(link, way).start()

            link_down = s - CHAIN_START - DOWN_START

            @pl.when(on_chain & (z == 0) & (link_down >= 0) & (link_down < CHAIN_CHUNKS))
            def _():
                @pl.when(link_down == 0)
                def _():
                    pl.semaphore_wait(chain_ready_down, 1)

                chain_copy(link_down, 1).start()

            @pl.when(s == flush_slot)
            def _():
                first_flush.start()

            @pl.when(s == head_slot)
            def _():
                @pl.when(edge & (z == 3))
                def _():
                    pl.semaphore_wait(small_ready, 1)

                @pl.when(edge & (z == 6))
                def _():
                    pl.semaphore_wait(small_ready_down, 1)

                small_event(0)

            @pl.when(s == small_slot)
            def _():
                small_event(1)

            return carry

        lax.fori_loop(0, SLOTS, slot, 0)

        @pl.when(jnp.logical_not(on_chain))
        def _():
            def arrived(chunk, carry):
                chain_copy(chunk, 2).wait_recv()
                return carry

            lax.fori_loop(0, CHAIN_CHUNKS, arrived, 0)

    flushes = [
        pltpu.make_async_copy(src, dst, out_sem.at[i])
        for i, (src, dst) in enumerate(((small, small_out), (rowp.at[1], rowp_out.at[1]), (colp, colp_out)))]
    for flush in flushes:
        flush.start()

    for way in range(4):
        @pl.when(send_tree[way] >= 0)
        def _():
            def sent(chunk, carry):
                tree_copy(0, chunk, way).wait_send()
                return carry

            lax.fori_loop(0, TREE_CHUNKS, sent, 0)

    for way in range(3):
        @pl.when(chain_ways[way])
        def _():
            def sent(chunk, carry):
                chain_copy(chunk, way).wait_send()
                return carry

            lax.fori_loop(0, CHAIN_CHUNKS, sent, 0)

    for which in range(2):
        for condition, copies in small_groups(which):
            @pl.when(condition)
            def _():
                for copy in copies:
                    copy.wait_send()

    for flush in [first_flush] + flushes:
        flush.wait()


def halves(value):
    high = value.astype(jnp.bfloat16)
    return high, (value - high.astype(jnp.float32)).astype(jnp.bfloat16)


def product(left, right):
    (left_high, left_low), (right_high, right_low) = left, right

    def dot(a, b):
        return jnp.dot(a, b, preferred_element_type=jnp.float32)

    return dot(left_high, right_high) + (dot(left_low, right_high) + dot(left_high, right_low))


def block_matrix(a, b, c, d):
    return jnp.concatenate([jnp.concatenate([a, b], axis=1), jnp.concatenate([c, d], axis=1)], axis=0)


TILE = 256


def update(
    corr, fock, rowp_in, colp_in, small_in, over, transformed, panel, rowp, colp, small, cbuf, fbuf, pbuf,
    over_left, over_right, fock_left, fock_right, in_sem, out_sem, panel_sem,
):
    r, c = lax.axis_index("row"), lax.axis_index("col")
    pairs = (
        (small_in, small), (rowp_in.at[0], rowp.at[0]), (colp_in.at[0], colp.at[0]), (corr, cbuf),
        (rowp_in.at[1], rowp.at[1]), (colp_in.at[1], colp.at[1]), (fock, fbuf))
    loads = [pltpu.make_async_copy(src, dst, in_sem.at[i]) for i, (src, dst) in enumerate(pairs)]
    for load in loads:
        load.start()
    loads[0].wait()

    size = rowp.shape[2]
    width = colp.shape[3]
    row = lax.broadcasted_iota(jnp.int32, (LANES, LANES), 0)
    col = lax.broadcasted_iota(jnp.int32, (LANES, LANES), 1)
    rest = jnp.zeros((LANES - PANEL, LANES), jnp.float32)
    packed = jnp.concatenate([small[1], rest], axis=0)
    turned = packed.T
    inv_real = jnp.where(row >= col, packed, 0.0)
    inv_imag = jnp.where(row > col, turned, 0.0)
    inv_real_t = jnp.where(row <= col, turned, 0.0)
    inv_imag_t = jnp.where(row < col, packed, 0.0)
    right_adjoint = halves(block_matrix(inv_real_t, -inv_imag_t, inv_imag_t, inv_real_t))
    right_inverse = halves(block_matrix(inv_real, inv_imag, -inv_imag, inv_real))
    left_inverse = halves(block_matrix(inv_real, -inv_imag, inv_imag, inv_real))
    left_adjoint = halves(block_matrix(inv_real_t, inv_imag_t, -inv_imag_t, inv_real_t))

    gap = jnp.zeros((LANES - PANEL, width), jnp.float32)

    def top(which):
        return jnp.concatenate([colp[which, 0], gap, colp[which, 1], gap], axis=0)

    loads[1].wait()
    factor = product(halves(jnp.concatenate([rowp[0, 0], rowp[0, 1]], axis=1)), right_adjoint)
    pbuf[0] = factor[:, 0:LANES].T[0:PANEL]
    pbuf[1] = factor[:, LANES:2 * LANES].T[0:PANEL]
    panel_out = pltpu.make_async_copy(pbuf, panel, panel_sem)
    panel_out.start()
    over_left[0], over_left[1] = halves(factor)
    loads[2].wait()
    across = product(left_inverse, halves(top(0)))

    def right_side(value):
        real, imag = value[0:LANES], value[LANES:2 * LANES]
        return block_matrix(real, imag, -imag, real)

    over_right[0], over_right[1] = halves(right_side(across))

    out_copies = []

    def outer_tiles(left, right, buffer, target, which, sign):
        for tile in range(2 * width // TILE):
            part, cols = tile // (width // TILE), pl.ds(tile % (width // TILE) * TILE, TILE)
            columns = pl.ds(tile * TILE, TILE)
            piece = product((left[0], left[1]), (right[0, :, columns], right[1, :, columns]))
            old = buffer[part, :, cols]
            buffer[part, :, cols] = old + piece if sign > 0 else old - piece
            copy = pltpu.make_async_copy(buffer.at[part, :, cols], target.at[part, :, cols], out_sem.at[which, tile])
            copy.start()
            out_copies.append(copy)

    loads[3].wait()
    outer_tiles(over_left, over_right, cbuf, over, 0, -1)

    wide_row = lax.broadcasted_iota(jnp.int32, (size, 2 * LANES), 0) + r * size
    wide_lane = lax.broadcasted_iota(jnp.int32, (size, 2 * LANES), 1)
    unit = jnp.where((wide_row == wide_lane) & (wide_lane < PANEL), 1.0, 0.0)
    trans = product(halves(unit - factor), right_inverse)
    loads[4].wait()
    loads[5].wait()
    left_real = jnp.concatenate([trans[:, 0:LANES], rowp[1, 0]], axis=1)
    left_imag = jnp.concatenate([trans[:, LANES:2 * LANES], rowp[1, 1]], axis=1)
    for i, value in enumerate((left_real, left_imag, left_real + left_imag)):
        fock_left[0, i], fock_left[1, i] = halves(value)
    tall_row = lax.broadcasted_iota(jnp.int32, (2 * LANES, width), 0)
    tall_lane = lax.broadcasted_iota(jnp.int32, (2 * LANES, width), 1) + c * width
    unit = jnp.where((tall_row == tall_lane) & (tall_row < PANEL), 1.0, 0.0)
    trans_across = product(left_adjoint, halves(unit - across))

    packed = jnp.concatenate([small[0], rest], axis=0)
    turned = packed.T
    head_real = jnp.where(row >= col, packed, turned)
    head_imag = jnp.where(row < col, packed, jnp.where(row > col, -turned, 0.0))
    head = halves(block_matrix(head_real, -head_imag, head_imag, head_real))
    middle = top(1) + product(head, halves(trans_across))
    right_real = jnp.concatenate([middle[0:LANES], trans_across[0:LANES]], axis=0)
    right_imag = jnp.concatenate([middle[LANES:2 * LANES], trans_across[LANES:2 * LANES]], axis=0)
    for i, value in enumerate((right_real, right_imag, right_real + right_imag)):
        fock_right[0, i], fock_right[1, i] = halves(value)

    loads[6].wait()
    for tile in range(width // TILE):
        cols = pl.ds(tile * TILE, TILE)
        first, second, third = (
            product((fock_left[0, i], fock_left[1, i]), (fock_right[0, i, :, cols], fock_right[1, i, :, cols])) for i in range(3))
        fbuf[0, :, cols] = fbuf[0, :, cols] + (first - second)
        fbuf[1, :, cols] = fbuf[1, :, cols] + ((third - first) - second)
        for part in range(2):
            copy = pltpu.make_async_copy(fbuf.at[part, :, cols], transformed.at[part, :, cols], out_sem.at[1, 2 * tile + part])
            copy.start()
            out_copies.append(copy)

    panel_out.wait()
    for copy in out_copies:
        copy.wait()


def shards(correlation, fock):
    rows, cols = correlation.shape[1:]
    f32, bf16 = jnp.float32, jnp.bfloat16
    hbm, vmem = pl.BlockSpec(memory_space=pl.ANY), pl.BlockSpec(memory_space=pltpu.VMEM)
    dma = pltpu.SemaphoreType.DMA
    rowp, colp, small = pl.pallas_call(
        spread,
        name="spread",
        out_shape=(
            jax.ShapeDtypeStruct((2, 2, rows, LANES), f32),
            jax.ShapeDtypeStruct((2, 2, PANEL, cols), f32),
            jax.ShapeDtypeStruct((2, PANEL, LANES), f32),
        ),
        in_specs=[hbm, hbm],
        out_specs=(hbm, hbm, hbm),
        scratch_shapes=[
            pltpu.VMEM((2, 2, rows, LANES), f32),
            pltpu.VMEM((2, 2, PANEL, cols), f32),
            pltpu.VMEM((2, PANEL, LANES), f32),
            pltpu.VMEM((PANEL, LANES), f32),
            pltpu.VMEM((LANES, LANES), f32),
            pltpu.VMEM((PANEL, LANES), f32),
            pltpu.VMEM((2, PANEL, LANES), f32),
            dma((5,)),
            dma((4,)),
            dma((4, TREE_CHUNKS)),
            dma((4, TREE_CHUNKS)),
            dma((3, CHAIN_CHUNKS)),
            dma((CHAIN_CHUNKS,)),
            dma((2, 12)),
            dma((2,)),
            pltpu.SemaphoreType.REGULAR,
            pltpu.SemaphoreType.REGULAR,
            pltpu.SemaphoreType.REGULAR,
            pltpu.SemaphoreType.REGULAR,
        ],
        compiler_params=pltpu.CompilerParams(collective_id=0, has_side_effects=True),
    )(correlation, fock)
    reduced, transformed, panel = pl.pallas_call(
        update,
        name="update",
        out_shape=(
            jax.ShapeDtypeStruct((2, rows, cols), f32),
            jax.ShapeDtypeStruct((2, rows, cols), f32),
            jax.ShapeDtypeStruct((2, PANEL, rows), f32),
        ),
        in_specs=[hbm, hbm, hbm, hbm, hbm],
        out_specs=(hbm, hbm, hbm),
        scratch_shapes=[
            pltpu.VMEM((2, 2, rows, LANES), f32),
            pltpu.VMEM((2, 2, PANEL, cols), f32),
            pltpu.VMEM((2, PANEL, LANES), f32),
            pltpu.VMEM((2, rows, cols), f32),
            pltpu.VMEM((2, rows, cols), f32),
            pltpu.VMEM((2, PANEL, rows), f32),
            pltpu.VMEM((2, rows, 2 * LANES), bf16),
            pltpu.VMEM((2, 2 * LANES, 2 * cols), bf16),
            pltpu.VMEM((2, 3, rows, 2 * LANES), bf16),
            pltpu.VMEM((2, 3, 2 * LANES, cols), bf16),
            dma((7,)),
            dma((2, 2 * cols // TILE)),
            dma,
        ],
        compiler_params=pltpu.CompilerParams(vmem_limit_bytes=65 * 1000 * 1000),
    )(correlation, fock, rowp, colp, small)
    return reduced, transformed, jnp.swapaxes(panel, 1, 2)


def solution(mesh):
    in_specs = (P(None, "row", "col"), P(None, "row", "col"))
    out_specs = (P(None, "row", "col"), P(None, "row", "col"), P(None, "row", None))
    return jax.shard_map(shards, mesh=mesh, in_specs=in_specs, out_specs=out_specs, check_vma=False)
```
